32 devices in a mesh: seq: 8 (over z, y), head: 4 (over x, core).
Axes of the slice: x: 2, y: 2, z: 4, core: 2. Of those that a mesh axis runs over, the one named last changes fastest.
Arguments:
- layer_input: bfloat16 [1, 1024, 1024], P(None, 'seq'), may hold values from -6 to 6
- first_layer_value: bfloat16 [1, 1024, 1024], P(None, 'seq', 'head'), may hold values from -6 to 6
- cotangent: bfloat16 [1, 1024, 1024], P(None, 'seq'), may hold values from -6 to 6
- receptance_weight: bfloat16 [1024, 1024], P('seq', 'head'), may hold values from -0.1875 to 0.1875
- key_weight: bfloat16 [1024, 1024], P('seq', 'head'), may hold values from -0.1875 to 0.1875
- value_weight: bfloat16 [1024, 1024], P('seq', 'head'), may hold values from -0.1875 to 0.1875
- output_weight: bfloat16 [1024, 1024], P('head', 'seq'), may hold values from -0.375 to 0.375
- channel_key_weight: bfloat16 [1024, 4096], P('seq', 'head'), may hold values from -0.1875 to 0.1875
- channel_value_weight: bfloat16 [4096, 1024], P('head', 'seq'), may hold values from -0.09375 to 0.09375
- decay_second_factor: bfloat16 [64, 1024], P('seq', 'head'), may hold values from -0.1875 to 0.1875
- learn_second_factor: bfloat16 [64, 1024], P('seq', 'head'), may hold values from -0.75 to 0.75
- residual_second_factor: bfloat16 [32, 1024], P('seq', 'head'), may hold values from -1 to 1
- gate_second_factor: bfloat16 [160, 1024], P('seq', 'head'), may hold values from -1 to 1
- decay_first_factor: bfloat16 [1024, 64], P(('seq', 'head')), may hold values from -0.1875 to 0.1875
- learn_first_factor: bfloat16 [1024, 64], P(('seq', 'head')), may hold values from -0.1875 to 0.1875
- residual_first_factor: bfloat16 [1024, 32], P(('seq', 'head')), may hold values from -0.1875 to 0.1875
- gate_first_factor: bfloat16 [1024, 160], P(('seq', 'head')), may hold values from -0.1875 to 0.1875
- vectors: float32 [1024, 19], P(('seq', 'head')), as said below
Outputs:
- result: float32 [1, 1024, 1024], P(None, 'seq', 'head')
- d_x_in: float32 [1, 1024, 1024], P(None, 'seq', 'head')
- d_v_first: float32 [1, 1024, 1024], P(None, 'seq', 'head')
- d_w_recept: float32 [1024, 1024], P('seq', 'head')
- d_w_key: float32 [1024, 1024], P('seq', 'head')
- d_w_value: float32 [1024, 1024], P('seq', 'head')
- d_w_out: float32 [1024, 1024], P('head', 'seq')
- d_w_ffn_key: float32 [1024, 4096], P('seq', 'head')
- d_w_ffn_value: float32 [4096, 1024], P('head', 'seq')
- d_lora_b_decay: float32 [64, 1024], P('seq', 'head')
- d_lora_b_iclr: float32 [64, 1024], P('seq', 'head')
- d_lora_b_mix: float32 [32, 1024], P('seq', 'head')
- d_lora_b_gate: float32 [160, 1024], P('seq', 'head')
- d_lora_a_decay: float32 [1024, 64], P(('seq', 'head'))
- d_lora_a_iclr: float32 [1024, 64], P(('seq', 'head'))
- d_lora_a_mix: float32 [1024, 32], P(('seq', 'head'))
- d_lora_a_gate: float32 [1024, 160], P(('seq', 'head'))
- d_vectors: float32 [1024, 19], P(('seq', 'head'))
The draws below stay inside these ranges and needn't reach their ends.
Inputs may be any that keep to these rules, and one draw needn't show every extreme that they name: Column c of vectors is one per-channel vector: 0 and 1 the first LayerNorm's gain (0.5 to 1.5) and bias (-0.5 to 0.5); 2 to 7 the token-shift mixes of receptance, decay, key, value, learning rate and gate (0 to 1); 8 the decay offset (log(0.3 / 1024) to 0); 9 the learning-rate offset (log(1 / 1024) to 1); 10 the value-residual offset (-1 to 1); 11 a key scaling (0.5 to 1.5); 12 a key scaling (0 to 1); 13 the bonus weights (-1 to 1); 14 and 15 the GroupNorm's gain and bias; 16 and 17 the second LayerNorm's gain and bias (ranges as for 0 and 1); 18 the channel mix's token-shift mix (0 to 1).
All inputs are finite; a program needn't handle non-finite values.
Results may differ from the reference program's by a relative error of at most 0.023.
Values may be sent and summed in bfloat16 or wider, within the bound.
No kernel may reach another device: no remote copies, remote signals or barrier semaphores. Data moves between devices by JAX's collectives and lax.ppermute only.
A program may use at most 128 MiB of HBM per device.

```python
import jax
import jax.numpy as jnp
from jax import lax

MODEL_WIDTH = 1024
HEAD = 64
FF = 4096
DECAY_RANK = 64
LEARN_RANK = 64
MIX_RANK = 32
GATE_RANK = 160
NV = 19
TOK_DEV = 128
SEQS = 1
LENGTH = 1024


def draw_vectors(key, part):
    subkeys = jax.random.split(key, 2)
    uniform_all = jax.random.uniform(subkeys[0], (MODEL_WIDTH, NV), jnp.float32)
    slow_heads = jax.random.bernoulli(subkeys[1], 0.5, (MODEL_WIDTH // HEAD,)).astype(jnp.float32)
    gains = 0.6 + 0.8 * uniform_all
    slow = jnp.repeat(slow_heads, HEAD)
    biases = uniform_all - 0.5
    spread = jnp.exp(jnp.log(10.0) * uniform_all[:, 8])
    decay_slow = jnp.log(0.3 * spread / LENGTH)
    decay_fast = -3.0 + 3.0 * uniform_all[:, 8]
    learn_slow = jnp.log((1.0 + 3.0 * uniform_all[:, 9]) / LENGTH)
    learn_fast = -2.0 + 3.0 * uniform_all[:, 9]
    decay_offset = slow * decay_slow + (1.0 - slow) * decay_fast
    learn_offset = slow * learn_slow + (1.0 - slow) * learn_fast
    columns = [gains[:, 0], biases[:, 1], uniform_all[:, 2], uniform_all[:, 3], uniform_all[:, 4], uniform_all[:, 5], uniform_all[:, 6], uniform_all[:, 7], decay_offset, learn_offset, 2.0 * uniform_all[:, 10] - 1.0, 0.5 + uniform_all[:, 11], uniform_all[:, 12], 2.0 * uniform_all[:, 13] - 1.0, gains[:, 14], biases[:, 15], gains[:, 16], biases[:, 17], uniform_all[:, 18]]
    return jnp.stack(columns, axis=1)


def levels(stream_key, extent, cuts, low, high):
    gain = 1.0
    for position, blocks in cuts:
        draws = jax.random.uniform(jax.random.fold_in(jax.random.fold_in(stream_key, 6), position), (blocks,), jnp.float32, low / len(cuts), high / len(cuts))
        gain = gain * jnp.repeat(jnp.exp(draws), extent[position] // blocks).reshape((-1,) + (1,) * (len(extent) - 1 - position))
    return gain


def noise(key, shape, scale, limit, shards=(), dtype=jnp.bfloat16):
    values = scale * jax.random.normal(key, shape, jnp.float32)
    if shards:
        values = values * levels(key, shape, shards, -0.22, 0.18)
    return jnp.clip(values, -limit, limit).astype(dtype)


def setup_inputs(seed: int = 0) -> dict:
    key_of = jax.random.split(jax.random.key(seed), 19)
    layer_input = noise(key_of[0], (SEQS, LENGTH, MODEL_WIDTH), 1.0, 6.0, ((1, 8),))
    first_layer_value = noise(key_of[1], (SEQS, LENGTH, MODEL_WIDTH), 1.0, 6.0, ((1, 8), (2, 4)))
    cotangent = noise(key_of[2], (SEQS, LENGTH, MODEL_WIDTH), 1.0, 6.0, ((1, 8),))
    receptance_weight = noise(key_of[3], (MODEL_WIDTH, MODEL_WIDTH), MODEL_WIDTH ** -0.5, 0.1875, ((0, 8), (1, 4)))
    key_weight = noise(key_of[4], (MODEL_WIDTH, MODEL_WIDTH), MODEL_WIDTH ** -0.5, 0.1875, ((0, 8), (1, 4)))
    value_weight = noise(key_of[5], (MODEL_WIDTH, MODEL_WIDTH), MODEL_WIDTH ** -0.5, 0.1875, ((0, 8), (1, 4)))
    output_weight = noise(key_of[6], (MODEL_WIDTH, MODEL_WIDTH), (MODEL_WIDTH // 4) ** -0.5, 0.375, ((0, 4), (1, 8)))
    channel_key_weight = noise(key_of[7], (MODEL_WIDTH, FF), MODEL_WIDTH ** -0.5, 0.1875, ((0, 8), (1, 4)))
    channel_value_weight = noise(key_of[8], (FF, MODEL_WIDTH), FF ** -0.5, 0.09375, ((0, 4), (1, 8)))
    decay_second_factor = noise(key_of[9], (DECAY_RANK, MODEL_WIDTH), (DECAY_RANK * 16) ** -0.5, 0.1875, ((0, 8), (1, 4)))
    learn_second_factor = noise(key_of[10], (LEARN_RANK, MODEL_WIDTH), LEARN_RANK ** -0.5, 0.75, ((0, 8), (1, 4)))
    residual_second_factor = noise(key_of[11], (MIX_RANK, MODEL_WIDTH), MIX_RANK ** -0.5, 1.0, ((0, 8), (1, 4)))
    gate_second_factor = noise(key_of[12], (GATE_RANK, MODEL_WIDTH), (GATE_RANK // 4) ** -0.5, 1.0, ((0, 8), (1, 4)))
    decay_first_factor = noise(key_of[13], (MODEL_WIDTH, DECAY_RANK), MODEL_WIDTH ** -0.5, 0.1875, ((0, 32),))
    learn_first_factor = noise(key_of[14], (MODEL_WIDTH, LEARN_RANK), MODEL_WIDTH ** -0.5, 0.1875, ((0, 32),))
    residual_first_factor = noise(key_of[15], (MODEL_WIDTH, MIX_RANK), MODEL_WIDTH ** -0.5, 0.1875, ((0, 32),))
    gate_first_factor = noise(key_of[16], (MODEL_WIDTH, GATE_RANK), MODEL_WIDTH ** -0.5, 0.1875, ((0, 32),))
    vectors = draw_vectors(jax.random.fold_in(key_of[18], 71), 0)
    return {"layer_input": layer_input, "first_layer_value": first_layer_value, "cotangent": cotangent, "receptance_weight": receptance_weight, "key_weight": key_weight, "value_weight": value_weight, "output_weight": output_weight, "channel_key_weight": channel_key_weight, "channel_value_weight": channel_value_weight, "decay_second_factor": decay_second_factor, "learn_second_factor": learn_second_factor, "residual_second_factor": residual_second_factor, "gate_second_factor": gate_second_factor, "decay_first_factor": decay_first_factor, "learn_first_factor": learn_first_factor, "residual_first_factor": residual_first_factor, "gate_first_factor": gate_first_factor, "vectors": vectors}


NORM_EPS = 1e-05
GROUP_EPS = 0.00064
UNIT_EPS = 1e-06
DECAY_SCALE = 0.606531
HIGHEST = lax.Precision.HIGHEST

def narrow_dot(former, latter):
    return jnp.dot(former.astype(jnp.bfloat16), latter.astype(jnp.bfloat16), preferred_element_type=jnp.float32)

def exact_dot(former, latter):
    return jnp.dot(former, latter, precision=HIGHEST)

def layer_norm(values, gain_column, bias_column):
    average = lax.optimization_barrier(jnp.mean(values, axis=-1, keepdims=True))
    centred = values - average
    spread = lax.optimization_barrier(jnp.mean(centred * centred, axis=-1, keepdims=True))
    return centred * lax.rsqrt(spread + NORM_EPS) * gain_column + bias_column

def first_norm(values, vectors):
    return layer_norm(values, vectors[:, 0], vectors[:, 1])

def second_norm(values, vectors):
    return layer_norm(values, vectors[:, 16], vectors[:, 17])

def shift_mix(standardized_signal, previous, weights):
    shifted = jnp.concatenate([previous[..., None, :], standardized_signal[..., :-1, :]], axis=-2)
    difference = shifted - standardized_signal
    return tuple((standardized_signal + difference * weights[:, column] for column in range(weights.shape[1])))

def time_inputs(standardized_signal, previous, vectors):
    return shift_mix(standardized_signal, previous, vectors[:, 2:8])

def ffn_inputs(standardized_signal, previous, vectors):
    return shift_mix(standardized_signal, previous, vectors[:, 18:19])[0]

def head_params(key_raw, value_raw, decay_shift, learn_shift, mix_shift, first_value, feedforward_sublevel):
    decays = jnp.exp(-DECAY_SCALE * jax.nn.sigmoid(feedforward_sublevel[:, 8] + decay_shift))
    learn_rate = jax.nn.sigmoid(feedforward_sublevel[:, 9] + learn_shift)
    content_shift_portion = value_raw + (first_value - value_raw) * jax.nn.sigmoid(feedforward_sublevel[:, 10] + mix_shift)
    scaled = key_raw * feedforward_sublevel[:, 11]
    parameter_arrangement = scaled.shape
    grouped = scaled.reshape(parameter_arrangement[:-1] + (parameter_arrangement[-1] // HEAD, HEAD))
    unit_keys = (grouped * lax.rsqrt(lax.optimization_barrier(jnp.sum(grouped * grouped, axis=-1, keepdims=True)) + UNIT_EPS)).reshape(parameter_arrangement)
    lookup_shift_portion = key_raw * (1.0 + (learn_rate - 1.0) * feedforward_sublevel[:, 12])
    return (decays, lookup_shift_portion, content_shift_portion, -unit_keys, unit_keys * learn_rate)

def head_output(memory_out, acceptance_matrix_lines, lookup_shift_portion, content_shift_portion, gates, feedforward_sublevel):
    parameter_arrangement = memory_out.shape
    partition_sizes_list = parameter_arrangement[:-1] + (parameter_arrangement[-1] // HEAD, HEAD)
    grouped = memory_out.reshape(partition_sizes_list)
    average = lax.optimization_barrier(jnp.mean(grouped, axis=-1, keepdims=True))
    centred = grouped - average
    spread = lax.optimization_barrier(jnp.mean(centred * centred, axis=-1, keepdims=True))
    standardized_signal = (centred * lax.rsqrt(spread + GROUP_EPS)).reshape(parameter_arrangement) * feedforward_sublevel[:, 14] + feedforward_sublevel[:, 15]
    current_token_extra = lax.optimization_barrier(jnp.sum((acceptance_matrix_lines * lookup_shift_portion * feedforward_sublevel[:, 13]).reshape(partition_sizes_list), axis=-1, keepdims=True))
    standardized_signal = standardized_signal + (current_token_extra * content_shift_portion.reshape(partition_sizes_list)).reshape(parameter_arrangement)
    return standardized_signal * gates

def transit(memory, decays, remover, refill):
    along = jnp.einsum('bvk,bk->bv', memory, remover, precision=HIGHEST)
    return memory * decays[:, None, :] + along[:, :, None] * refill[:, None, :]

def step_state(memory, decays, remover, refill, key_row, value_row):
    return transit(memory, decays, remover, refill) + value_row[:, :, None] * key_row[:, None, :]

def run_forward(initial, blocked, keep_states):

    def advance(memory, inputs):
        updated = step_state(memory, inputs[0], inputs[1], inputs[2], inputs[3], inputs[4])
        output = jnp.einsum('bvk,bk->bv', updated, inputs[5], precision=HIGHEST)
        if keep_states:
            return (updated, (memory, output))
        return (updated, output)
    return lax.scan(advance, initial, blocked)

def run_backward(gradient, before, blocked, grad_rows):

    def retreat(carried, inputs):
        memory, decays, remover, refill, key_row, value_row, recept_row, grad_row = inputs
        updated = step_state(memory, decays, remover, refill, key_row, value_row)
        carried = carried + grad_row[:, :, None] * recept_row[:, None, :]
        recept_grad = jnp.einsum('bvk,bv->bk', updated, grad_row, precision=HIGHEST)
        value_grad = jnp.einsum('bvk,bk->bv', carried, key_row, precision=HIGHEST)
        key_grad = jnp.einsum('bvk,bv->bk', carried, value_row, precision=HIGHEST)
        decay_grad = lax.optimization_barrier(jnp.sum(carried * memory, axis=1))
        along = jnp.einsum('bvk,bk->bv', memory, remover, precision=HIGHEST)
        refill_grad = jnp.einsum('bvk,bv->bk', carried, along, precision=HIGHEST)
        along_grad = jnp.einsum('bvk,bk->bv', carried, refill, precision=HIGHEST)
        remover_grad = jnp.einsum('bvk,bv->bk', memory, along_grad, precision=HIGHEST)
        carried = carried * decays[:, None, :] + along_grad[:, :, None] * remover[:, None, :]
        return (carried, (decay_grad, remover_grad, refill_grad, key_grad, value_grad, recept_grad))
    return lax.scan(retreat, gradient, (before,) + tuple(blocked) + (grad_rows,), reverse=True)

def one_sequence(x_row, first_row, cot_row, weight_matrices, vectors):
    recept_cols, key_cols, value_cols, out_rows, ffn_key_cols, ffn_value_rows, decay_up, learn_up, mix_up, gate_up, decay_down, learn_down, mix_down, gate_down = weight_matrices
    values = x_row.astype(jnp.float32)
    length, features = values.shape
    head_count = features // HEAD
    blocks = length // TOK_DEV
    zero_row = jnp.zeros((features,), jnp.float32)

    def attn_path(inputs, vecs):
        return time_inputs(first_norm(inputs, vecs), zero_row, vecs)

    def ffn_path(inputs, vecs):
        return ffn_inputs(second_norm(inputs, vecs), zero_row, vecs)
    mixed_recept, mixed_decay, mixed_key, mixed_value, mixed_learn, mixed_gate = attn_path(values, vectors)
    acceptance_matrix_lines = narrow_dot(mixed_recept, recept_cols)
    key_raw = narrow_dot(mixed_key, key_cols)
    value_raw = narrow_dot(mixed_value, value_cols)
    decay_low = narrow_dot(mixed_decay, decay_down)
    learn_low = narrow_dot(mixed_learn, learn_down)
    mix_low = narrow_dot(mixed_value, mix_down)
    gate_low = narrow_dot(mixed_gate, gate_down)
    decay_tanh = jnp.tanh(decay_low)
    gate_sigm = jax.nn.sigmoid(gate_low)
    decay_shift = narrow_dot(decay_tanh, decay_up)
    learn_shift = narrow_dot(learn_low, learn_up)
    mix_shift = narrow_dot(mix_low, mix_up)
    gates = narrow_dot(gate_sigm, gate_up)
    first_value = first_row.astype(jnp.float32)
    decays, lookup_shift_portion, content_shift_portion, remover, refill = head_params(key_raw, value_raw, decay_shift, learn_shift, mix_shift, first_value, vectors)
    blocked = tuple((member.reshape(blocks, TOK_DEV, head_count, HEAD) for member in (decays, remover, refill, lookup_shift_portion, content_shift_portion, acceptance_matrix_lines)))
    zero_state = jnp.zeros((head_count, HEAD, HEAD), jnp.float32)

    def block_forward(memory, block_in):
        last_state, outputs = run_forward(memory, block_in, False)
        return (last_state, (memory, outputs))
    _, (starts, outputs) = lax.scan(block_forward, zero_state, blocked)
    memory_out = outputs.reshape(length, features)
    pre_out = head_output(memory_out, acceptance_matrix_lines, lookup_shift_portion, content_shift_portion, gates, vectors)
    middle = values + narrow_dot(pre_out, out_rows)
    mixed_ffn = ffn_path(middle, vectors)
    hidden_pre = narrow_dot(mixed_ffn, ffn_key_cols)
    active = jnp.maximum(hidden_pre, 0.0)
    hidden = active * active
    result = middle + narrow_dot(hidden, ffn_value_rows)
    grad_ffn_value = narrow_dot(hidden.T, cot_row)
    pre_grad = narrow_dot(cot_row, ffn_value_rows.T) * 2.0 * active
    grad_ffn_key = narrow_dot(mixed_ffn.T, pre_grad)
    mixed_ffn_grad = narrow_dot(pre_grad, ffn_key_cols.T)
    _, ffn_back = jax.vjp(ffn_path, middle, vectors)
    middle_part, vec_ffn = ffn_back(mixed_ffn_grad)
    middle_grad = cot_row.astype(jnp.float32) + middle_part
    grad_out = narrow_dot(pre_out.T, middle_grad)
    pre_out_grad = narrow_dot(middle_grad, out_rows.T)
    _, output_back = jax.vjp(head_output, memory_out, acceptance_matrix_lines, lookup_shift_portion, content_shift_portion, gates, vectors)
    memory_grad, recept_part, key_part, value_part, gate_grad, vec_out = output_back(pre_out_grad)
    grad_gate_up = narrow_dot(gate_sigm.T, gate_grad)
    gate_low_grad = narrow_dot(gate_grad, gate_up.T) * gate_sigm * (1.0 - gate_sigm)
    grad_blocks = memory_grad.reshape(blocks, TOK_DEV, head_count, HEAD)

    def block_backward(gradient, block_in):
        memory, member, grad_block = block_in
        _, (before, _) = run_forward(memory, member, True)
        return run_backward(gradient, before, member, grad_block)
    _, chain_grads = lax.scan(block_backward, zero_state, (starts, blocked, grad_blocks), reverse=True)
    decay_grad, remover_grad, refill_grad, key_chain, value_chain, recept_chain = [member.reshape(length, features) for member in chain_grads]
    _, param_back = jax.vjp(head_params, key_raw, value_raw, decay_shift, learn_shift, mix_shift, first_value, vectors)
    key_grad, value_grad, decay_shift_grad, learn_shift_grad, mix_shift_grad, first_grad, vec_param = param_back((decay_grad, key_part + key_chain, value_part + value_chain, remover_grad, refill_grad))
    recept_grad = recept_part + recept_chain
    grad_decay_up = narrow_dot(decay_tanh.T, decay_shift_grad)
    decay_low_grad = narrow_dot(decay_shift_grad, decay_up.T) * (1.0 - decay_tanh * decay_tanh)
    grad_learn_up = narrow_dot(learn_low.T, learn_shift_grad)
    learn_low_grad = narrow_dot(learn_shift_grad, learn_up.T)
    grad_mix_up = narrow_dot(mix_low.T, mix_shift_grad)
    mix_low_grad = narrow_dot(mix_shift_grad, mix_up.T)
    decay_wide = decay_down.astype(jnp.float32)
    learn_wide = learn_down.astype(jnp.float32)
    mix_wide = mix_down.astype(jnp.float32)
    gate_wide = gate_down.astype(jnp.float32)
    grad_decay_down = exact_dot(mixed_decay.T, decay_low_grad)
    grad_learn_down = exact_dot(mixed_learn.T, learn_low_grad)
    grad_mix_down = exact_dot(mixed_value.T, mix_low_grad)
    grad_gate_down = exact_dot(mixed_gate.T, gate_low_grad)
    grad_recept = narrow_dot(mixed_recept.T, recept_grad)
    grad_key = narrow_dot(mixed_key.T, key_grad)
    grad_value = narrow_dot(mixed_value.T, value_grad)
    mixes_grad = (narrow_dot(recept_grad, recept_cols.T), exact_dot(decay_low_grad, decay_wide.T), narrow_dot(key_grad, key_cols.T), narrow_dot(value_grad, value_cols.T) + exact_dot(mix_low_grad, mix_wide.T), exact_dot(learn_low_grad, learn_wide.T), exact_dot(gate_low_grad, gate_wide.T))
    _, attn_back = jax.vjp(attn_path, values, vectors)
    input_part, vec_attn = attn_back(mixes_grad)
    input_grad = middle_grad + input_part
    grad_vectors = vec_ffn + vec_out + vec_param + vec_attn
    return ((result, input_grad, first_grad), (grad_recept, grad_key, grad_value, grad_out, grad_ffn_key, grad_ffn_value, grad_decay_up, grad_learn_up, grad_mix_up, grad_gate_up, grad_decay_down, grad_learn_down, grad_mix_down, grad_gate_down, grad_vectors))

def reference(layer_input, first_layer_value, cotangent, receptance_weight, key_weight, value_weight, output_weight, channel_key_weight, channel_value_weight, decay_second_factor, learn_second_factor, residual_second_factor, gate_second_factor, decay_first_factor, learn_first_factor, residual_first_factor, gate_first_factor, vectors):
    weight_matrices = (receptance_weight, key_weight, value_weight, output_weight, channel_key_weight, channel_value_weight, decay_second_factor, learn_second_factor, residual_second_factor, gate_second_factor, decay_first_factor, learn_first_factor, residual_first_factor, gate_first_factor)
    zeros = tuple((jnp.zeros(member.shape, jnp.float32) for member in weight_matrices)) + (jnp.zeros(vectors.shape, jnp.float32),)

    def sequence_step(totals, inputs):
        outputs, grads = one_sequence(inputs[0], inputs[1], inputs[2], weight_matrices, vectors)
        return (tuple((total + grad_term for total, grad_term in zip(totals, grads))), outputs)
    grads, (result, input_grad, first_grad) = lax.scan(sequence_step, zeros, (layer_input, first_layer_value, cotangent))
    return (result, input_grad, first_grad, grads[0], grads[1], grads[2], grads[3], grads[4], grads[5], grads[6], grads[7], grads[8], grads[9], grads[10], grads[11], grads[12], grads[13], grads[14])
```

```python
import functools


import jax
import jax.numpy as jnp
from jax import lax
from jax.experimental import pallas as pl
from jax.sharding import PartitionSpec as P

HEAD = 64
CHUNK = 64
INTERPRET = False

NORM_EPS = 1e-05
GROUP_EPS = 0.00064
UNIT_EPS = 1e-06
DECAY_SCALE = 0.606531
BF16 = jnp.bfloat16
F32 = jnp.float32


def shifted_route(axis, distance):
    devices = range(lax.axis_size(axis))
    return [(i, i + distance) for i in devices if i + distance in devices]


def ring_route(axis, distance):
    size = lax.axis_size(axis)
    return [(i, (i + distance) % size) for i in range(size)]


def head_sum(partial_value):
    sent = partial_value.astype(BF16)
    total = partial_value
    for distance in range(1, lax.axis_size("head")):
        total = total + lax.ppermute(sent, "head", ring_route("head", distance)).astype(F32)
    return total


def head_scatter(partial_value, kind=BF16):
    size, place = (lax.axis_size("head"), lax.axis_index("head"))
    width = partial_value.shape[1] // size
    sent = partial_value.astype(kind)
    total = lax.dynamic_slice_in_dim(partial_value, place * width, width, 1)
    for distance in range(1, size):
        block = lax.dynamic_slice_in_dim(sent, (place + distance) % size * width, width, 1)
        total = total + lax.ppermute(block, "head", ring_route("head", distance)).astype(F32)
    return total


def permute_gather(rows, axis):
    size, place = (lax.axis_size(axis), lax.axis_index(axis))
    count = rows.shape[0]
    whole = jnp.zeros((size * count, rows.shape[1]), rows.dtype)
    whole = lax.dynamic_update_slice_in_dim(whole, rows, place * count, 0)
    for distance in range(1, size):
        block = lax.ppermute(rows, axis, ring_route(axis, distance))
        whole = lax.dynamic_update_slice_in_dim(
            whole, block, (place - distance) % size * count, 0
        )
    return whole


def after(value, other):
    never = lax.axis_index("seq") >= lax.axis_size("seq")
    return jnp.where(never, other[(0,) * other.ndim].astype(value.dtype), value)


def stack(parts, axis):
    total = sum(part.shape[axis] for part in parts)
    whole = None
    at = 0
    for part in parts:
        size = part.shape[axis]
        edges = [(0, 0, 0)] * part.ndim
        edges[axis] = (at, total - at - size, 0)
        padded = lax.pad(part, jnp.zeros((), part.dtype), edges)
        whole = padded if whole is None else whole + padded
        at += size
    return whole


def share_out(rows):
    tokens, features = rows.shape
    size = lax.axis_size("seq")
    return rows.reshape(tokens, size, features // size).transpose(1, 0, 2)


def split_three(values):
    high = lax.reduce_precision(values, 8, 7)
    rest = values - high
    middle = lax.reduce_precision(rest, 8, 7)
    return (high.astype(BF16), middle.astype(BF16), (rest - middle).astype(BF16))


def narrow_dot(former, latter):
    return jnp.dot(former.astype(BF16), latter.astype(BF16), preferred_element_type=F32)


def narrow_tn(former, latter):
    return lax.dot_general(
        former.astype(BF16),
        latter.astype(BF16),
        (((0,), (0,)), ((), ())),
        preferred_element_type=F32,
    )


def narrow_nt(former, latter):
    return lax.dot_general(
        former.astype(BF16),
        latter.astype(BF16),
        (((1,), (1,)), ((), ())),
        preferred_element_type=F32,
    )


def standardize(values):
    average = jnp.mean(values, axis=-1, keepdims=True)
    centred = values - average
    spread = jnp.mean(centred * centred, axis=-1, keepdims=True)
    return centred * lax.rsqrt(spread + NORM_EPS)


def layer_norm(values, gain_row, bias_row):
    return standardize(values) * gain_row + bias_row


def shift_mix(normed, previous, weights):
    shifted = jnp.concatenate([previous, normed[:-1]], axis=0)
    difference = shifted - normed
    return tuple((normed + difference * weights[c] for c in range(weights.shape[0])))


def head_sums(values):
    width = values.shape[1]
    return jnp.concatenate(
        [
            jnp.broadcast_to(
                jnp.sum(values[:, at : at + HEAD], axis=1, keepdims=True),
                (values.shape[0], HEAD),
            )
            for at in range(0, width, HEAD)
        ],
        axis=1,
    )


def head_params(refs):
    key_raw, value_raw, decay_shift, learn_shift, mix_shift, first_value = (
        ref[...].astype(F32) for ref in refs[:6]
    )
    table = refs[6]
    decay_gate = jax.nn.sigmoid(table[8:9] + decay_shift)
    rate = jax.nn.sigmoid(table[9:10] + learn_shift)
    mixing = jax.nn.sigmoid(table[10:11] + mix_shift)
    content = value_raw + (first_value - value_raw) * mixing
    scaled_key = key_raw * table[11:12]
    size = lax.rsqrt(head_sums(scaled_key * scaled_key) + UNIT_EPS)
    unit = scaled_key * size
    slope = 1.0 + (rate - 1.0) * table[12:13]
    return dict(
        key_raw=key_raw,
        decay_gate=decay_gate,
        rate=rate,
        mixing=mixing,
        gap=first_value - value_raw,
        size=size,
        unit=unit,
        slope=slope,
        decay_log=-DECAY_SCALE * decay_gate,
        remover=-unit,
        refill=unit * rate,
        key=key_raw * slope,
        content=content,
    )


def head_output(memory, recept, key, content, gates, table):
    centred = memory - head_sums(memory) / HEAD
    spread = lax.rsqrt(head_sums(centred * centred) / HEAD + GROUP_EPS)
    standard = centred * spread
    extra = head_sums(recept * key * table[13:14])
    shown = standard * table[14:15] + table[15:16] + extra * content
    return dict(spread=spread, standard=standard, extra=extra, shown=shown, out=shown * gates)


def token_sum(values):
    return jnp.sum(values, axis=0, keepdims=True)


def split_two(x):
    high = x.astype(BF16)
    return (high, (x - high.astype(F32)).astype(BF16))


NN = (((1,), (0,)), ((), ()))
NT = (((1,), (1,)), ((), ()))
TN = (((0,), (0,)), ((), ()))


def mm(x, y, dims=NN, passes=3):
    def dot(p, q):
        return lax.dot_general(p, q, dims, preferred_element_type=F32)

    if passes == 1:
        return dot(x.astype(BF16), y.astype(BF16))
    xh, xl = split_two(x)
    yh, yl = split_two(y)
    return dot(xh, yh) + (dot(xh, yl) + dot(xl, yh))


def cumulate(mask, x, dims=NN):
    ones = mask.astype(F32).astype(BF16)
    high = x.astype(BF16)
    rest = x - high.astype(F32)
    middle = rest.astype(BF16)
    low = (rest - middle.astype(F32)).astype(BF16)

    def dot(q):
        return lax.dot_general(ones, q, dims, preferred_element_type=F32)

    return dot(high) + (dot(middle) + dot(low))


def masks(tokens, chunk):
    row = lax.broadcasted_iota(jnp.int32, (tokens, tokens), 0)
    col = lax.broadcasted_iota(jnp.int32, (tokens, tokens), 1)
    same = (row // chunk) == (col // chunk)
    strict = same & (col < row)
    inclusive = same & (col <= row)
    return row, col, same, strict, inclusive


def unit_inverse(lower, row, col, chunk):
    eye = jnp.where(row == col, 1.0, 0.0).astype(F32)
    base = min(16, chunk)
    diagonal = jnp.where((row // base) == (col // base), lower, 0.0)
    inverse = eye + diagonal
    power = diagonal
    reach = 2
    while reach < base:
        power = mm(power, power)
        inverse = inverse + mm(inverse, power)
        reach *= 2
    size = base
    while size < chunk:
        size *= 2
        across = jnp.where(
            ((row // size) == (col // size)) & ((row // (size // 2)) != (col // (size // 2))),
            lower,
            0.0,
        )
        inverse = inverse + mm(inverse, mm(across, inverse))
    return inverse


def scaled(decay_log, inclusive, same):
    total = cumulate(inclusive, decay_log)
    ending = cumulate(same, decay_log)
    before = total - decay_log
    return dict(
        ending=ending,
        e_before=jnp.exp(before),
        e_total=jnp.exp(total),
        e_back=jnp.exp(-total),
        e_end=jnp.exp(ending - total),
    )


def head_pieces(ah, rh, bi, ki, v, geometry, chunk):
    row, col, _, strict, inclusive = geometry
    tokens = ah.shape[0]
    pairs = mm(jnp.concatenate([ah, rh], axis=0), jnp.concatenate([bi, ki], axis=0), NT)
    ab = jnp.where(strict, pairs[:tokens, :tokens], 0.0)
    ak = jnp.where(strict, pairs[:tokens, tokens:], 0.0)
    rb = jnp.where(inclusive, pairs[tokens:, :tokens], 0.0)
    rk = jnp.where(inclusive, pairs[tokens:, tokens:], 0.0)
    reads = jnp.concatenate([rb, rk], axis=1)
    inverse = unit_inverse(ab, row, col, chunk)
    u = mm(inverse, mm(ak, v))
    w = mm(inverse, ah)
    reader = rh + mm(rb, w)
    uv = jnp.concatenate([u, v], axis=0)
    base = mm(reads, uv)
    return dict(ak=ak, rb=rb, reads=reads, inverse=inverse, u=u, w=w, uv=uv, reader=reader, base=base)


def head_states(p, be, ke, v, scale, chunk):
    tokens = v.shape[0]
    r64 = lax.broadcasted_iota(jnp.int32, (HEAD, HEAD), 0)
    c64 = lax.broadcasted_iota(jnp.int32, (HEAD, HEAD), 1)
    out = []
    for at in range(0, tokens, chunk):
        s = slice(at, at + chunk)
        diagonal = jnp.where(r64 == c64, jnp.broadcast_to(scale[at : at + 1], (HEAD, HEAD)), 0.0)
        transition = diagonal + mm(p["w"][s], be[s], TN)
        fresh = mm(p["u"][s], be[s], TN) + mm(v[s], ke[s], TN)
        out.append((transition, fresh))
    return out


def members_of(refs):
    p = head_params(refs)
    return p, (
        p["decay_log"], p["remover"], p["refill"], p["key"], p["content"], refs[7][...]
    )


def local_kernel(chunk, *refs):
    tf_ref, rd_ref, ba_ref, sent_ref = refs[RAWS:]
    tokens, width = rd_ref.shape
    geometry = masks(tokens, chunk)
    same, inclusive = (geometry[2], geometry[4])
    decay_log, a, b, k, v, r = members_of(refs[:RAWS])[1]
    e = scaled(decay_log, inclusive, same)
    full = (
        a * e["e_before"],
        r * e["e_total"],
        b * e["e_back"],
        k * e["e_back"],
        b * e["e_end"],
        k * e["e_end"],
        v,
        jnp.exp(e["ending"]),
    )
    for h in range(width // HEAD):
        lanes = slice(h * HEAD, (h + 1) * HEAD)
        ah, rh, bi, ki, be, ke, vh, scale = (x[:, lanes] for x in full)
        p = head_pieces(ah, rh, bi, ki, vh, geometry, chunk)
        rd_ref[:, lanes] = p["reader"]
        ba_ref[:, lanes] = p["base"]
        states = head_states(p, be, ke, vh, scale, chunk)
        total_t = total_f = None
        for c, (transition, fresh) in enumerate(states):
            tf_ref[h, c, :, :HEAD] = transition
            tf_ref[h, c, :, HEAD:] = fresh
            if c == 0:
                total_t, total_f = (transition, fresh)
            else:
                total_f = mm(total_f, transition) + fresh
                total_t = mm(total_t, transition)
        sent_ref[h, :, :HEAD] = total_f.astype(BF16)
        sent_ref[h, :, HEAD:] = total_t.astype(BF16)


def outputs_kernel(count, chunk, *refs):
    got = refs[:count]
    raws = refs[count : count + RAWS]
    tf_ref, rd_ref, ba_ref, gates_ref, out_ref, pre_ref, initial_ref = refs[count + RAWS :]
    tokens, width = rd_ref.shape
    for h in range(width // HEAD):
        lanes = slice(h * HEAD, (h + 1) * HEAD)
        state = jnp.zeros((HEAD, HEAD), F32)
        for g in got:
            state = mm(state, g[h, :, HEAD:].astype(F32)) + g[h, :, :HEAD].astype(F32)
        initial_ref[h] = state
        for c in range(tokens // chunk):
            s = slice(c * chunk, (c + 1) * chunk)
            out_ref[s, lanes] = mm(rd_ref[s, lanes], state, NT) + ba_ref[s, lanes]
            if c + 1 < tokens // chunk:
                state = mm(state, tf_ref[h, c, :, :HEAD]) + tf_ref[h, c, :, HEAD:]
    p = head_params(raws)
    o = head_output(out_ref[...], raws[7][...], p["key"], p["content"], gates_ref[...], raws[6])
    pre_ref[...] = o["out"].astype(BF16)


def local_back_kernel(chunk, *refs):
    raws = refs[:RAWS]
    (
        tf_ref, rd_ref, upper_ref, memory_ref, gates_ref, sent_ref,
        back_ref, g_ref, recept_ref, key_ref, value_ref, gate_ref, table_ref,
    ) = refs[RAWS:]
    tokens, width = rd_ref.shape
    table, recept = (raws[6], raws[7][...])
    p = head_params(raws)
    o = head_output(memory_ref[...], recept, p["key"], p["content"], gates_ref[...], table)
    upper = upper_ref[...]
    gate_ref[...] = (upper * o["shown"]).astype(BF16)
    dshown = upper * gates_ref[...]
    dstandard = dshown * table[14:15]
    g_ref[...] = o["spread"] * (
        dstandard
        - head_sums(dstandard) / HEAD
        - o["standard"] * (head_sums(dstandard * o["standard"]) / HEAD)
    )
    dextra = head_sums(dshown * p["content"])
    value_ref[...] = dshown * o["extra"]
    recept_ref[...] = dextra * p["key"] * table[13:14]
    key_ref[...] = dextra * recept * table[13:14]
    table_ref[0:1] = token_sum(dextra * recept * p["key"])
    table_ref[1:2] = token_sum(dshown * o["standard"])
    table_ref[2:3] = token_sum(dshown)
    for h in range(width // HEAD):
        lanes = slice(h * HEAD, (h + 1) * HEAD)
        grad = None
        for c in reversed(range(tokens // chunk)):
            s = slice(c * chunk, (c + 1) * chunk)
            own = mm(g_ref[s, lanes], rd_ref[s, lanes], TN)
            grad = own if grad is None else mm(grad, tf_ref[h, c, :, :HEAD], NT) + own
        back_ref[h, :, :HEAD] = grad.astype(BF16)
        back_ref[h, :, HEAD:] = sent_ref[h, :, HEAD:]


def back_kernel(count, chunk, *refs):
    got = refs[:count]
    raws = refs[count : count + RAWS]
    (
        initial_ref, tf_ref, rd_ref, g_ref, recept_ref, key_ref, value_ref,
        dr_ref, dk_ref, dv_ref, ddecay_ref, dlearn_ref, dmix_ref, first_ref, table_ref,
    ) = refs[count + RAWS :]
    tokens, width = rd_ref.shape
    chunks = tokens // chunk
    geometry = masks(tokens, chunk)
    _, _, same, strict, inclusive = geometry
    r64 = lax.broadcasted_iota(jnp.int32, (HEAD, HEAD), 0)
    c64 = lax.broadcasted_iota(jnp.int32, (HEAD, HEAD), 1)
    raw, (decay_log, a, b, k, v, r) = members_of(raws)
    e = scaled(decay_log, inclusive, same)
    ah_f, rh_f, bi_f, ki_f, be_f, ke_f = (
        a * e["e_before"],
        r * e["e_total"],
        b * e["e_back"],
        k * e["e_back"],
        b * e["e_end"],
        k * e["e_end"],
    )
    scale_f = jnp.exp(e["ending"])
    dah_l, drh_l, dbi_l, dki_l, dbe_l, dke_l, dv_l, dend_l = ([] for _ in range(8))
    for h in range(width // HEAD):
        lanes = slice(h * HEAD, (h + 1) * HEAD)
        ah, rh, bi, ki, be, ke, vh, _ = (
            x[:, lanes] for x in (ah_f, rh_f, bi_f, ki_f, be_f, ke_f, v, scale_f)
        )
        g = g_ref[:, lanes]
        p = head_pieces(ah, rh, bi, ki, vh, geometry, chunk)
        u, w = (p["u"], p["w"])
        starts = [initial_ref[h]]
        for c in range(chunks - 1):
            starts.append(mm(starts[c], tf_ref[h, c, :, :HEAD]) + tf_ref[h, c, :, HEAD:])
        grad = jnp.zeros((HEAD, HEAD), F32)
        for m in got:
            grad = mm(grad, m[h, :, HEAD:].astype(F32), NT) + m[h, :, :HEAD].astype(F32)
        nexts = [None] * chunks
        for c in reversed(range(chunks)):
            nexts[c] = grad
            if c:
                s = slice(c * chunk, (c + 1) * chunk)
                grad = mm(grad, tf_ref[h, c, :, :HEAD], NT) + mm(g[s], rd_ref[s, lanes], TN)
        dw, du, dv, dbe, dke, dreader, dend = ([] for _ in range(7))
        for c in range(chunks):
            s = slice(c * chunk, (c + 1) * chunk)
            dt = mm(starts[c], nexts[c], TN)
            df = nexts[c]
            dreader.append(mm(g[s], starts[c]))
            dw.append(mm(be[s], dt, NT))
            du.append(mm(be[s], df, NT))
            dv.append(mm(ke[s], df, NT))
            dbe.append(mm(w[s], dt) + mm(u[s], df))
            dke.append(mm(vh[s], df))
            line = jnp.sum(jnp.where(r64 == c64, dt, 0.0), axis=0, keepdims=True)
            dend.append(jnp.broadcast_to(line, (chunk, HEAD)))
        dw, du, dv, dbe, dke, dreader, dend = (
            jnp.concatenate(x, axis=0) for x in (dw, du, dv, dbe, dke, dreader, dend)
        )
        dreads = mm(g, p["uv"], NT)
        drb = jnp.where(inclusive, mm(dreader, w, NT) + dreads[:, :tokens], 0.0)
        drk = jnp.where(inclusive, dreads[:, tokens:], 0.0)
        duv = mm(p["reads"], g, TN)
        dw = dw + mm(p["rb"], dreader, TN)
        du = du + duv[:tokens]
        dz = mm(p["inverse"], du, TN)
        q = mm(p["inverse"], dw, TN)
        dsolve = mm(dz, p["uv"], NT)
        dab = jnp.where(strict, mm(q, w, NT) + dsolve[:, :tokens], 0.0)
        dak = jnp.where(strict, dsolve[:, tokens:], 0.0)
        dv = dv + duv[tokens:] + mm(p["ak"], dz, TN)
        dpairs = jnp.concatenate(
            [jnp.concatenate([dab, dak], axis=1), jnp.concatenate([drb, drk], axis=1)], axis=0
        )
        dleft = mm(dpairs, jnp.concatenate([bi, ki], axis=0))
        dright = mm(dpairs, jnp.concatenate([ah, rh], axis=0), TN)
        dah_l.append(q + dleft[:tokens])
        drh_l.append(dreader + dleft[tokens:])
        dbi_l.append(dright[:tokens])
        dki_l.append(dright[tokens:])
        dbe_l.append(dbe)
        dke_l.append(dke)
        dv_l.append(dv)
        dend_l.append(dend)
    dah, drh, dbi, dki, dbe, dke, dv, dend = (
        jnp.concatenate(x, axis=1)
        for x in (dah_l, drh_l, dbi_l, dki_l, dbe_l, dke_l, dv_l, dend_l)
    )
    da = dah * e["e_before"]
    dr = drh * e["e_total"] + recept_ref[...]
    db = dbi * e["e_back"] + dbe * e["e_end"]
    dk = dki * e["e_back"] + dke * e["e_end"] + key_ref[...]
    dv = dv + value_ref[...]
    dbefore = dah * ah_f
    at_end = dbe * be_f + dke * ke_f
    dtotal = dbefore + drh * rh_f - dbi * bi_f - dki * ki_f - at_end
    dl = cumulate(inclusive, dtotal, TN) - dbefore + cumulate(same, at_end) + dend * scale_f
    table = raws[6]
    key_raw, rate, mixing, unit = (raw["key_raw"], raw["rate"], raw["mixing"], raw["unit"])
    ddecay = dl * (-DECAY_SCALE) * raw["decay_gate"] * (1.0 - raw["decay_gate"])
    dslope = dk * key_raw
    dlearn = (db * unit + dslope * table[12:13]) * rate * (1.0 - rate)
    dmix = dv * raw["gap"] * mixing * (1.0 - mixing)
    dunit = db * rate - da
    dscaled = raw["size"] * (dunit - unit * head_sums(dunit * unit))
    first_ref[...] = dv * mixing
    dr_ref[...] = dr.astype(BF16)
    dk_ref[...] = (dscaled * table[11:12] + dk * raw["slope"]).astype(BF16)
    dv_ref[...] = (dv * (1.0 - mixing)).astype(BF16)
    ddecay_ref[...] = ddecay.astype(BF16)
    dlearn_ref[...] = dlearn.astype(BF16)
    dmix_ref[...] = dmix.astype(BF16)
    table_ref[0:1] = token_sum(ddecay)
    table_ref[1:2] = token_sum(dlearn)
    table_ref[2:3] = token_sum(dmix)
    table_ref[3:4] = token_sum(dscaled * key_raw)
    table_ref[4:5] = token_sum(dslope * (rate - 1.0))


RAWS = 8


def chunk_of(tokens):
    return min(tokens, CHUNK)


def pairs_of(channels):
    return 2 if channels % (2 * HEAD) == 0 else channels // HEAD


def wkv_call(kernel, channels, inputs, outs):
    group = pairs_of(channels)
    width = group * HEAD

    def spec(shape):
        if len(shape) == 2:
            return pl.BlockSpec((shape[0], width), lambda i: (0, i))
        rest = tuple(shape[1:])
        return pl.BlockSpec((group,) + rest, lambda i: (i,) + (0,) * len(rest))

    return pl.pallas_call(
        kernel,
        grid=(channels // width,),
        in_specs=[spec(x.shape) for x in inputs],
        out_specs=[spec(s) for s, _ in outs],
        out_shape=[jax.ShapeDtypeStruct(s, d) for s, d in outs],
        interpret=INTERPRET,
    )(*inputs)


def wkv_local(raws):
    tokens, channels = raws[0].shape
    heads, chunk = (channels // HEAD, chunk_of(tokens))
    return wkv_call(
        functools.partial(local_kernel, chunk),
        channels,
        raws,
        [
            ((heads, tokens // chunk, HEAD, 2 * HEAD), F32),
            ((tokens, channels), F32),
            ((tokens, channels), F32),
            ((heads, HEAD, 2 * HEAD), BF16),
        ],
    )


def wkv_outputs(got, raws, tf, reader, base, gates):
    tokens, channels = reader.shape
    heads, chunk = (channels // HEAD, chunk_of(tokens))
    return wkv_call(
        functools.partial(outputs_kernel, len(got), chunk),
        channels,
        [*got, *raws, tf, reader, base, gates],
        [
            ((tokens, channels), F32),
            ((tokens, channels), BF16),
            ((heads, HEAD, HEAD), F32),
        ],
    )


def wkv_local_back(raws, tf, reader, upper, memory, gates, sent):
    tokens, channels = reader.shape
    return wkv_call(
        functools.partial(local_back_kernel, chunk_of(tokens)),
        channels,
        [*raws, tf, reader, upper, memory, gates, sent],
        [(sent.shape, BF16)]
        + [((tokens, channels), F32)] * 4
        + [((tokens, channels), BF16), ((3, channels), F32)],
    )


def wkv_back(got, raws, initial, tf, reader, grad, parts):
    tokens, channels = reader.shape
    return wkv_call(
        functools.partial(back_kernel, len(got), chunk_of(tokens)),
        channels,
        [*got, *raws, initial, tf, reader, grad, *parts],
        [
            *[((tokens, channels), BF16)] * 6,
            ((tokens, channels), F32),
            ((5, channels), F32),
        ],
    )


def state_exchange(values, distance_sign):
    size = lax.axis_size("seq")
    return [
        lax.ppermute(values, "seq", shifted_route("seq", distance_sign * distance))
        for distance in range(size - 1, 0, -1)
    ]


def body(
    layer_input,
    first_layer_value,
    cotangent,
    receptance_weight,
    key_weight,
    value_weight,
    output_weight,
    channel_key_weight,
    channel_value_weight,
    decay_second_factor,
    learn_second_factor,
    residual_second_factor,
    gate_second_factor,
    decay_first_factor,
    learn_first_factor,
    residual_first_factor,
    gate_first_factor,
    vectors,
):
    sequences, tokens, features = layer_input.shape
    assert sequences == 1
    channels = first_layer_value.shape[2]
    hidden_units = channel_key_weight.shape[1]
    seq_size, seq_place = (lax.axis_size("seq"), lax.axis_index("seq"))
    head_size, head_place = (lax.axis_size("head"), lax.axis_index("head"))
    offset = head_place * channels
    share = features // seq_size
    small_share = features // (seq_size * head_size)

    x_bf = layer_input.reshape(tokens, features)
    x_rows = x_bf.astype(F32)
    cot_bf = cotangent.reshape(tokens, features)
    previous_x = lax.ppermute(x_bf[-1:], "seq", shifted_route("seq", 1)).astype(F32)
    has_previous = (seq_place > 0).astype(F32)

    firsts = (decay_first_factor, learn_first_factor, residual_first_factor, gate_first_factor)
    ranks = [member.shape[1] for member in firsts]
    columns = vectors.shape[1]
    small = jnp.concatenate(firsts + split_three(vectors), axis=1)
    seconds = (
        decay_second_factor,
        learn_second_factor,
        residual_second_factor,
        gate_second_factor,
    )
    second_rows = [member.shape[0] for member in seconds]
    payload = stack(
        [receptance_weight, key_weight, value_weight, output_weight.T, *seconds], 0
    )
    gathered = lax.all_gather(payload, "seq", axis=0, tiled=False)
    cuts = []
    at = 0
    for rows in [share] * 4 + second_rows:
        cuts.append(gathered[:, at : at + rows].reshape(seq_size * rows, channels))
        at += rows
    recept_cols, key_cols, value_cols, out_cols, decay_up, learn_up, mix_up, gate_up = cuts

    shared = lax.all_to_all(
        jnp.concatenate([share_out(standardize(x_rows).astype(BF16)), share_out(cot_bf)], axis=2),
        "seq",
        split_axis=0,
        concat_axis=0,
        tiled=True,
    )
    standard_all = shared[..., :share].reshape(seq_size * tokens, share)
    cot_all = shared[..., share:].reshape(seq_size * tokens, share)

    small_all = permute_gather(after(small, payload), "seq")
    small_all = permute_gather(small_all, "head")
    small_all = (
        small_all.reshape(head_size, seq_size, small_share, -1)
        .transpose(1, 0, 2, 3)
        .reshape(features, -1)
    )
    downs = []
    at = 0
    for rank in ranks:
        downs.append(small_all[:, at : at + rank])
        at += rank
    decay_down, learn_down, mix_down, gate_down = downs
    pieces = small_all[:, at : at + 3 * columns].astype(F32)
    vec = (
        pieces[:, :columns] + pieces[:, columns : 2 * columns] + pieces[:, 2 * columns :]
    ).T
    local_vec = lax.dynamic_slice_in_dim(vec, offset, channels, 1)

    ffn_payload = after(
        jnp.concatenate([channel_key_weight, channel_value_weight.T], axis=1), shared
    )
    ffn_gathered = lax.all_gather(ffn_payload, "seq", axis=0, tiled=True)
    ffn_key_cols = ffn_gathered[:, :hidden_units]
    ffn_value_cols = ffn_gathered[:, hidden_units:]

    def first_norm(values, table):
        return layer_norm(values, table[0], table[1])

    def second_norm(values, table):
        return layer_norm(values, table[16], table[17])

    def time_inputs(normed, previous, table):
        return shift_mix(normed, previous, table[2:8])

    def ffn_inputs(normed, previous, table):
        return shift_mix(normed, previous, table[18:19])[0]

    normed_a = first_norm(x_rows, vec)
    prev_a = first_norm(previous_x, vec) * has_previous
    mixes = time_inputs(normed_a, prev_a, vec)
    mixed_recept, mixed_decay, mixed_key, mixed_value, mixed_learn, mixed_gate = mixes
    recept = narrow_dot(mixed_recept, recept_cols)
    key_raw = narrow_dot(mixed_key, key_cols)
    value_raw = narrow_dot(mixed_value, value_cols)
    decay_low = narrow_dot(mixed_decay, decay_down)
    learn_low = narrow_dot(mixed_learn, learn_down)
    mix_low = narrow_dot(mixed_value, mix_down)
    gate_low = narrow_dot(mixed_gate, gate_down)
    decay_tanh = jnp.tanh(decay_low)
    gate_sigm = jax.nn.sigmoid(gate_low)
    decay_shift = narrow_dot(decay_tanh, decay_up)
    learn_shift = narrow_dot(learn_low, learn_up)
    mix_shift = narrow_dot(mix_low, mix_up)
    gates = narrow_dot(gate_sigm, gate_up)
    first_value = first_layer_value.reshape(tokens, channels)
    raws = (
        key_raw, value_raw, decay_shift, learn_shift, mix_shift, first_value, local_vec, recept
    )
    states, reader, base, sent = wkv_local(raws)
    memory_out, pre_out, initial = wkv_outputs(
        state_exchange(sent, 1), raws, states, reader, base, gates
    )
    middle = x_rows + head_sum(narrow_nt(pre_out, out_cols))
    normed_b, norm_b_back = jax.vjp(second_norm, middle, vec)
    prev_b = lax.ppermute(normed_b[-1:], "seq", shifted_route("seq", 1))
    mixed_ffn, ffn_back = jax.vjp(ffn_inputs, normed_b, prev_b, vec)
    middle_share = lax.dynamic_slice_in_dim(middle, offset, channels, 1)
    hidden_pre = narrow_dot(mixed_ffn, ffn_key_cols)
    active = jnp.maximum(hidden_pre, 0.0)
    hidden = active * active
    result = middle_share + head_scatter(narrow_nt(hidden, ffn_value_cols))
    pre_grad = narrow_dot(cot_bf, ffn_value_cols) * 2.0 * active
    ffn_rows = lax.all_gather(
        jnp.concatenate([member.astype(BF16) for member in (hidden, pre_grad, pre_out)], axis=1),
        "seq",
        axis=0,
        tiled=True,
    )
    ffn_back_part = narrow_nt(pre_grad, ffn_key_cols)
    normed_b_grad, prev_b_grad, vec_ffn_mix = ffn_back(ffn_back_part)
    returned_b = lax.ppermute(prev_b_grad, "seq", shifted_route("seq", -1))
    normed_b_grad = jnp.concatenate([normed_b_grad[:-1], normed_b_grad[-1:] + returned_b], axis=0)
    middle_part, vec_ffn_norm = norm_b_back(normed_b_grad)
    middle_grad = cot_bf.astype(F32) + head_sum(middle_part)
    middle_grad_share = lax.dynamic_slice_in_dim(middle_grad, offset, channels, 1)
    pre_out_grad = narrow_dot(middle_grad, out_cols)
    sent_back, memory_grad, recept_part, key_part, value_part, gate_grad, table_out = (
        wkv_local_back(raws, states, reader, pre_out_grad, memory_out, gates, sent)
    )
    grad_gate_up = narrow_tn(gate_sigm, gate_grad)
    gate_low_grad = narrow_nt(gate_grad, gate_up) * gate_sigm * (1.0 - gate_sigm)
    *row_grads, first_grad, table_param = wkv_back(
        state_exchange(sent_back, -1),
        raws,
        initial,
        states,
        reader,
        memory_grad,
        (recept_part, key_part, value_part),
    )
    decay_shift_grad, learn_shift_grad, mix_shift_grad = row_grads[3:]
    decay_low_grad = narrow_nt(decay_shift_grad, decay_up) * (1.0 - decay_tanh * decay_tanh)
    learn_low_grad = narrow_nt(learn_shift_grad, learn_up)
    mix_low_grad = narrow_nt(mix_shift_grad, mix_up)
    low_grad = head_sum(
        jnp.concatenate([decay_low_grad, learn_low_grad, mix_low_grad, gate_low_grad], axis=1)
    )
    final = jnp.concatenate(
        [*row_grads[:3], low_grad.astype(BF16)], axis=1
    )
    sent_final = after(final, ffn_rows)
    final = lax.all_gather(sent_final, "seq", axis=0, tiled=True)
    second_grads = (
        narrow_tn(decay_tanh, after(decay_shift_grad, sent_final)),
        narrow_tn(learn_low, after(learn_shift_grad, sent_final)),
        narrow_tn(mix_low, after(mix_shift_grad, sent_final)),
        grad_gate_up,
    )
    second_parts = []
    for member, rows in zip(second_grads, second_rows):
        member = member.astype(BF16).reshape(seq_size, rows, channels)
        second_parts += [member[..., at : at + share] for at in range(0, channels, share)]
    recept_sent, key_sent, value_sent = (
        sent_final[:, c * channels : (c + 1) * channels] for c in range(3)
    )
    mixes_grad = (
        narrow_nt(recept_sent, recept_cols),
        narrow_nt(after(decay_low_grad, sent_final), decay_down),
        narrow_nt(key_sent, key_cols),
        narrow_nt(value_sent, value_cols) + narrow_nt(after(mix_low_grad, sent_final), mix_down),
        narrow_nt(after(learn_low_grad, sent_final), learn_down),
        narrow_nt(after(gate_low_grad, sent_final), gate_down),
    )
    _, mix_back = jax.vjp(time_inputs, normed_a, prev_a, vec)
    normed_a_grad, prev_a_grad, vec_attn_mix = mix_back(mixes_grad)
    returned_a = lax.ppermute(prev_a_grad, "seq", shifted_route("seq", -1))
    normed_a_grad = jnp.concatenate([normed_a_grad[:-1], normed_a_grad[-1:] + returned_a], axis=0)
    _, norm_a_back = jax.vjp(first_norm, x_rows, vec)
    input_part, vec_attn_norm = norm_a_back(normed_a_grad)
    input_grad = middle_grad_share + head_scatter(input_part)

    table_local = jnp.concatenate([table_param, table_out], axis=0)
    vec_grad = lax.dynamic_update_slice(
        vec_ffn_mix + vec_ffn_norm + vec_attn_mix + vec_attn_norm, table_local, (8, offset)
    )
    vec_split = vec_grad.reshape(columns, seq_size, share).transpose(1, 0, 2)
    vec_high, vec_low, _ = split_three(vec_split)
    last = lax.all_to_all(
        stack(
            [share_out(mixed_ffn.astype(BF16)), share_out(middle_grad.astype(BF16))]
            + [*second_parts, vec_high, vec_low],
            1,
        ),
        "seq",
        split_axis=0,
        concat_axis=0,
        tiled=True,
    )
    mixed_all = last[:, :tokens].reshape(seq_size * tokens, share)
    middle_grad_all = last[:, tokens : 2 * tokens].reshape(seq_size * tokens, share)
    sums = jnp.sum(last[:, 2 * tokens :].astype(F32), axis=0)
    second_sum = sums[: -2 * columns]
    vec_seq = sums[-2 * columns : -columns] + sums[-columns:]
    vec_mine = head_scatter(vec_seq, F32).T

    share_vec = lax.dynamic_slice_in_dim(vec, seq_place * share, share, 1)
    normed_all = standard_all.astype(F32) * share_vec[0] + share_vec[1]
    zero_row = jnp.zeros((1, share), F32)
    recept_all, decay_all, key_all, value_all, learn_all, gate_all = shift_mix(
        normed_all, zero_row, share_vec[2:8]
    )
    grad_recept = narrow_tn(recept_all, final[:, :channels])
    grad_key = narrow_tn(key_all, final[:, channels : 2 * channels])
    grad_value = narrow_tn(value_all, final[:, 2 * channels : 3 * channels])
    first_outs = []
    at = 3 * channels
    for member, rank in zip((decay_all, learn_all, value_all, gate_all), ranks):
        mine = lax.dynamic_slice_in_dim(member, head_place * small_share, small_share, 1)
        first_outs.append(narrow_tn(mine, final[:, at : at + rank]))
        at += rank

    hidden_all = ffn_rows[:, :hidden_units]
    pre_grad_all = ffn_rows[:, hidden_units : 2 * hidden_units]
    pre_out_all = ffn_rows[:, 2 * hidden_units :]
    second_outs = []
    at = 0
    for rows in second_rows:
        parts = []
        for _ in range(0, channels, share):
            parts.append(second_sum[at : at + rows])
            at += rows
        second_outs.append(jnp.concatenate(parts, axis=1))
    return (
        result[None],
        input_grad[None],
        first_grad[None],
        grad_recept,
        grad_key,
        grad_value,
        narrow_tn(pre_out_all, middle_grad_all),
        narrow_tn(mixed_all, pre_grad_all),
        narrow_tn(hidden_all, cot_all),
        *second_outs,
        *first_outs,
        vec_mine,
    )


def solution(mesh):
    placed = (
        P(None, "seq", None),
        P(None, "seq", "head"),
        P(None, "seq", None),
        P("seq", "head"),
        P("seq", "head"),
        P("seq", "head"),
        P("head", "seq"),
        P("seq", "head"),
        P("head", "seq"),
        P("seq", "head"),
        P("seq", "head"),
        P("seq", "head"),
        P("seq", "head"),
        P(("seq", "head"), None),
        P(("seq", "head"), None),
        P(("seq", "head"), None),
        P(("seq", "head"), None),
        P(("seq", "head"), None),
    )
    return jax.shard_map(
        body,
        mesh=mesh,
        in_specs=placed,
        out_specs=(
            P(None, "seq", "head"),
            P(None, "seq", "head"),
            P(None, "seq", "head"),
            P("seq", "head"),
            P("seq", "head"),
            P("seq", "head"),
            P("head", "seq"),
            P("seq", "head"),
            P("head", "seq"),
            P("seq", "head"),
            P("seq", "head"),
            P("seq", "head"),
            P("seq", "head"),
            P(("seq", "head"), None),
            P(("seq", "head"), None),
            P(("seq", "head"), None),
            P(("seq", "head"), None),
            P(("seq", "head"), None),
        ),
        check_vma=False,
    )
```

```python
import functools


import jax
import jax.numpy as jnp
from jax import lax
from jax.experimental import pallas as pl
from jax.sharding import PartitionSpec as P

HEAD = 64
CHUNK = 64
INTERPRET = False

NORM_EPS = 1e-05
GROUP_EPS = 0.00064
UNIT_EPS = 1e-06
DECAY_SCALE = 0.606531
BF16 = jnp.bfloat16
F32 = jnp.float32


def shifted_route(axis, distance):
    devices = range(lax.axis_size(axis))
    return [(i, i + distance) for i in devices if i + distance in devices]


def ring_route(axis, distance):
    size = lax.axis_size(axis)
    return [(i, (i + distance) % size) for i in range(size)]


def head_sum(partial_value):
    sent = partial_value.astype(BF16)
    total = partial_value
    for distance in range(1, lax.axis_size("head")):
        total = total + lax.ppermute(sent, "head", ring_route("head", distance)).astype(F32)
    return total


def head_scatter(partial_value, kind=BF16):
    size, place = (lax.axis_size("head"), lax.axis_index("head"))
    width = partial_value.shape[1] // size
    sent = partial_value.astype(kind)
    total = lax.dynamic_slice_in_dim(partial_value, place * width, width, 1)
    for distance in range(1, size):
        block = lax.dynamic_slice_in_dim(sent, (place + distance) % size * width, width, 1)
        total = total + lax.ppermute(block, "head", ring_route("head", distance)).astype(F32)
    return total


def permute_gather(rows, axis):
    size, place = (lax.axis_size(axis), lax.axis_index(axis))
    count = rows.shape[0]
    whole = jnp.zeros((size * count, rows.shape[1]), rows.dtype)
    whole = lax.dynamic_update_slice_in_dim(whole, rows, place * count, 0)
    for distance in range(1, size):
        block = lax.ppermute(rows, axis, ring_route(axis, distance))
        whole = lax.dynamic_update_slice_in_dim(
            whole, block, (place - distance) % size * count, 0
        )
    return whole


def after(value, other):
    never = lax.axis_index("seq") >= lax.axis_size("seq")
    return jnp.where(never, other[(0,) * other.ndim].astype(value.dtype), value)


def stack(parts, axis):
    total = sum(part.shape[axis] for part in parts)
    whole = None
    at = 0
    for part in parts:
        size = part.shape[axis]
        edges = [(0, 0, 0)] * part.ndim
        edges[axis] = (at, total - at - size, 0)
        padded = lax.pad(part, jnp.zeros((), part.dtype), edges)
        whole = padded if whole is None else whole + padded
        at += size
    return whole


def share_out(rows):
    tokens, features = rows.shape
    size = lax.axis_size("seq")
    return rows.reshape(tokens, size, features // size).transpose(1, 0, 2)


def split_three(values):
    high = lax.reduce_precision(values, 8, 7)
    rest = values - high
    middle = lax.reduce_precision(rest, 8, 7)
    return (high.astype(BF16), middle.astype(BF16), (rest - middle).astype(BF16))


def narrow_dot(former, latter):
    return jnp.dot(former.astype(BF16), latter.astype(BF16), preferred_element_type=F32)


def narrow_tn(former, latter):
    return lax.dot_general(
        former.astype(BF16),
        latter.astype(BF16),
        (((0,), (0,)), ((), ())),
        preferred_element_type=F32,
    )


def narrow_nt(former, latter):
    return lax.dot_general(
        former.astype(BF16),
        latter.astype(BF16),
        (((1,), (1,)), ((), ())),
        preferred_element_type=F32,
    )


def standardize(values):
    average = jnp.mean(values, axis=-1, keepdims=True)
    centred = values - average
    spread = jnp.mean(centred * centred, axis=-1, keepdims=True)
    return centred * lax.rsqrt(spread + NORM_EPS)


def layer_norm(values, gain_row, bias_row):
    return standardize(values) * gain_row + bias_row


def shift_mix(normed, previous, weights):
    shifted = jnp.concatenate([previous, normed[:-1]], axis=0)
    difference = shifted - normed
    return tuple((normed + difference * weights[c] for c in range(weights.shape[0])))


def head_sums(values):
    width = values.shape[1]
    return jnp.concatenate(
        [
            jnp.broadcast_to(
                jnp.sum(values[:, at : at + HEAD], axis=1, keepdims=True),
                (values.shape[0], HEAD),
            )
            for at in range(0, width, HEAD)
        ],
        axis=1,
    )


def head_params(refs):
    key_raw, value_raw, decay_shift, learn_shift, mix_shift, first_value = (
        ref[...].astype(F32) for ref in refs[:6]
    )
    table = refs[6]
    decay_gate = jax.nn.sigmoid(table[8:9] + decay_shift)
    rate = jax.nn.sigmoid(table[9:10] + learn_shift)
    mixing = jax.nn.sigmoid(table[10:11] + mix_shift)
    content = value_raw + (first_value - value_raw) * mixing
    scaled_key = key_raw * table[11:12]
    size = lax.rsqrt(head_sums(scaled_key * scaled_key) + UNIT_EPS)
    unit = scaled_key * size
    slope = 1.0 + (rate - 1.0) * table[12:13]
    return dict(
        key_raw=key_raw,
        decay_gate=decay_gate,
        rate=rate,
        mixing=mixing,
        gap=first_value - value_raw,
        size=size,
        unit=unit,
        slope=slope,
        decay_log=-DECAY_SCALE * decay_gate,
        remover=-unit,
        refill=unit * rate,
        key=key_raw * slope,
        content=content,
    )


def head_output(memory, recept, key, content, gates, table):
    centred = memory - head_sums(memory) / HEAD
    spread = lax.rsqrt(head_sums(centred * centred) / HEAD + GROUP_EPS)
    standard = centred * spread
    extra = head_sums(recept * key * table[13:14])
    shown = standard * table[14:15] + table[15:16] + extra * content
    return dict(spread=spread, standard=standard, extra=extra, shown=shown, out=shown * gates)


def token_sum(values):
    return jnp.sum(values, axis=0, keepdims=True)


def split_two(x):
    high = x.astype(BF16)
    return (high, (x - high.astype(F32)).astype(BF16))


NN = (((1,), (0,)), ((), ()))
NT = (((1,), (1,)), ((), ()))
TN = (((0,), (0,)), ((), ()))


def mm(x, y, dims=NN, passes=3):
    def dot(p, q):
        return lax.dot_general(p, q, dims, preferred_element_type=F32)

    if passes == 1:
        return dot(x.astype(BF16), y.astype(BF16))
    xh, xl = split_two(x)
    yh, yl = split_two(y)
    return dot(xh, yh) + (dot(xh, yl) + dot(xl, yh))


def mm1(x, y, dims=NN):
    return mm(x, y, dims, 1)


def cumulate(mask, x, dims=NN):
    ones = mask.astype(F32).astype(BF16)
    high = x.astype(BF16)
    rest = x - high.astype(F32)
    middle = rest.astype(BF16)
    low = (rest - middle.astype(F32)).astype(BF16)

    def dot(q):
        return lax.dot_general(ones, q, dims, preferred_element_type=F32)

    return dot(high) + (dot(middle) + dot(low))


def masks(tokens, chunk):
    row = lax.broadcasted_iota(jnp.int32, (tokens, tokens), 0)
    col = lax.broadcasted_iota(jnp.int32, (tokens, tokens), 1)
    same = (row // chunk) == (col // chunk)
    strict = same & (col < row)
    inclusive = same & (col <= row)
    return row, col, same, strict, inclusive


def unit_inverse(lower, row, col, chunk):
    eye = jnp.where(row == col, 1.0, 0.0).astype(F32)
    base = min(16, chunk)
    diagonal = jnp.where((row // base) == (col // base), lower, 0.0)
    inverse = eye + diagonal
    power = diagonal
    reach = 2
    while reach < base:
        power = mm(power, power)
        inverse = inverse + mm(inverse, power)
        reach *= 2
    size = base
    while size < chunk:
        size *= 2
        across = jnp.where(
            ((row // size) == (col // size)) & ((row // (size // 2)) != (col // (size // 2))),
            lower,
            0.0,
        )
        inverse = inverse + mm(inverse, mm(across, inverse))
    return inverse


def scaled(decay_log, inclusive, same):
    total = cumulate(inclusive, decay_log)
    ending = cumulate(same, decay_log)
    before = total - decay_log
    return dict(
        ending=ending,
        e_before=jnp.exp(before),
        e_total=jnp.exp(total),
        e_back=jnp.exp(-total),
        e_end=jnp.exp(ending - total),
    )


def head_pieces(ah, rh, bi, ki, v, geometry, chunk):
    row, col, _, strict, inclusive = geometry
    tokens = ah.shape[0]
    pairs = mm(jnp.concatenate([ah, rh], axis=0), jnp.concatenate([bi, ki], axis=0), NT)
    ab = jnp.where(strict, pairs[:tokens, :tokens], 0.0)
    ak = jnp.where(strict, pairs[:tokens, tokens:], 0.0)
    rb = jnp.where(inclusive, pairs[tokens:, :tokens], 0.0)
    rk = jnp.where(inclusive, pairs[tokens:, tokens:], 0.0)
    reads = jnp.concatenate([rb, rk], axis=1)
    inverse = unit_inverse(ab, row, col, chunk)
    u = mm(inverse, mm(ak, v))
    w = mm(inverse, ah)
    reader = rh + mm(rb, w)
    uv = jnp.concatenate([u, v], axis=0)
    base = mm(reads, uv)
    return dict(ak=ak, rb=rb, reads=reads, inverse=inverse, u=u, w=w, uv=uv, reader=reader, base=base)


def head_states(p, be, ke, v, scale, chunk):
    tokens = v.shape[0]
    r64 = lax.broadcasted_iota(jnp.int32, (HEAD, HEAD), 0)
    c64 = lax.broadcasted_iota(jnp.int32, (HEAD, HEAD), 1)
    out = []
    for at in range(0, tokens, chunk):
        s = slice(at, at + chunk)
        diagonal = jnp.where(r64 == c64, jnp.broadcast_to(scale[at : at + 1], (HEAD, HEAD)), 0.0)
        transition = diagonal + mm(p["w"][s], be[s], TN)
        fresh = mm(p["u"][s], be[s], TN) + mm(v[s], ke[s], TN)
        out.append((transition, fresh))
    return out


def members_of(refs):
    p = head_params(refs)
    return p, (
        p["decay_log"], p["remover"], p["refill"], p["key"], p["content"], refs[7][...]
    )


def local_kernel(chunk, *refs):
    tf_ref, rd_ref, ba_ref, sent_ref, saved_ref = refs[RAWS:]
    tokens, width = rd_ref.shape
    geometry = masks(tokens, chunk)
    same, inclusive = (geometry[2], geometry[4])
    decay_log, a, b, k, v, r = members_of(refs[:RAWS])[1]
    e = scaled(decay_log, inclusive, same)
    full = (
        a * e["e_before"],
        r * e["e_total"],
        b * e["e_back"],
        k * e["e_back"],
        b * e["e_end"],
        k * e["e_end"],
        v,
        jnp.exp(e["ending"]),
    )
    for h in range(width // HEAD):
        lanes = slice(h * HEAD, (h + 1) * HEAD)
        ah, rh, bi, ki, be, ke, vh, scale = (x[:, lanes] for x in full)
        p = head_pieces(ah, rh, bi, ki, vh, geometry, chunk)
        rd_ref[:, lanes] = p["reader"]
        ba_ref[:, lanes] = p["base"]
        saved_ref[h, :, :tokens] = p["inverse"]
        saved_ref[h, :, tokens : 2 * tokens] = p["ak"]
        saved_ref[h, :, 2 * tokens : 4 * tokens] = p["reads"]
        saved_ref[h, :, 4 * tokens : 4 * tokens + HEAD] = p["u"]
        saved_ref[h, :, 4 * tokens + HEAD :] = p["w"]
        states = head_states(p, be, ke, vh, scale, chunk)
        total_t = total_f = None
        for c, (transition, fresh) in enumerate(states):
            tf_ref[h, c, :, :HEAD] = transition
            tf_ref[h, c, :, HEAD:] = fresh
            if c == 0:
                total_t, total_f = (transition, fresh)
            else:
                total_f = mm(total_f, transition) + fresh
                total_t = mm(total_t, transition)
        sent_ref[h, :, :HEAD] = total_f.astype(BF16)
        sent_ref[h, :, HEAD:] = total_t.astype(BF16)


def outputs_kernel(count, chunk, *refs):
    got = refs[:count]
    raws = refs[count : count + RAWS]
    tf_ref, rd_ref, ba_ref, gates_ref, out_ref, pre_ref, initial_ref = refs[count + RAWS :]
    tokens, width = rd_ref.shape
    for h in range(width // HEAD):
        lanes = slice(h * HEAD, (h + 1) * HEAD)
        state = jnp.zeros((HEAD, HEAD), F32)
        for g in got:
            state = mm(state, g[h, :, HEAD:].astype(F32)) + g[h, :, :HEAD].astype(F32)
        initial_ref[h] = state
        for c in range(tokens // chunk):
            s = slice(c * chunk, (c + 1) * chunk)
            out_ref[s, lanes] = mm(rd_ref[s, lanes], state, NT) + ba_ref[s, lanes]
            if c + 1 < tokens // chunk:
                state = mm(state, tf_ref[h, c, :, :HEAD]) + tf_ref[h, c, :, HEAD:]
    p = head_params(raws)
    o = head_output(out_ref[...], raws[7][...], p["key"], p["content"], gates_ref[...], raws[6])
    pre_ref[...] = o["out"].astype(BF16)


def local_back_kernel(chunk, *refs):
    raws = refs[:RAWS]
    (
        tf_ref, rd_ref, upper_ref, memory_ref, gates_ref, sent_ref,
        back_ref, g_ref, recept_ref, key_ref, value_ref, gate_ref, table_ref,
    ) = refs[RAWS:]
    tokens, width = rd_ref.shape
    table, recept = (raws[6], raws[7][...])
    p = head_params(raws)
    o = head_output(memory_ref[...], recept, p["key"], p["content"], gates_ref[...], table)
    upper = upper_ref[...]
    gate_ref[...] = (upper * o["shown"]).astype(BF16)
    dshown = upper * gates_ref[...]
    dstandard = dshown * table[14:15]
    g_ref[...] = o["spread"] * (
        dstandard
        - head_sums(dstandard) / HEAD
        - o["standard"] * (head_sums(dstandard * o["standard"]) / HEAD)
    )
    dextra = head_sums(dshown * p["content"])
    value_ref[...] = dshown * o["extra"]
    recept_ref[...] = dextra * p["key"] * table[13:14]
    key_ref[...] = dextra * recept * table[13:14]
    table_ref[0:1] = token_sum(dextra * recept * p["key"])
    table_ref[1:2] = token_sum(dshown * o["standard"])
    table_ref[2:3] = token_sum(dshown)
    for h in range(width // HEAD):
        lanes = slice(h * HEAD, (h + 1) * HEAD)
        grad = None
        for c in reversed(range(tokens // chunk)):
            s = slice(c * chunk, (c + 1) * chunk)
            own = mm(g_ref[s, lanes], rd_ref[s, lanes], TN)
            grad = own if grad is None else mm(grad, tf_ref[h, c, :, :HEAD], NT) + own
        back_ref[h, :, :HEAD] = grad.astype(BF16)
        back_ref[h, :, HEAD:] = sent_ref[h, :, HEAD:]


def back_kernel(count, chunk, *refs):
    got = refs[:count]
    raws = refs[count : count + RAWS]
    (
        initial_ref, tf_ref, rd_ref, g_ref, saved_ref, recept_ref, key_ref, value_ref,
        dr_ref, dk_ref, dv_ref, ddecay_ref, dlearn_ref, dmix_ref, first_ref, table_ref,
    ) = refs[count + RAWS :]
    tokens, width = rd_ref.shape
    chunks = tokens // chunk
    geometry = masks(tokens, chunk)
    _, _, same, strict, inclusive = geometry
    r64 = lax.broadcasted_iota(jnp.int32, (HEAD, HEAD), 0)
    c64 = lax.broadcasted_iota(jnp.int32, (HEAD, HEAD), 1)
    raw, (decay_log, a, b, k, v, r) = members_of(raws)
    e = scaled(decay_log, inclusive, same)
    ah_f, rh_f, bi_f, ki_f, be_f, ke_f = (
        a * e["e_before"],
        r * e["e_total"],
        b * e["e_back"],
        k * e["e_back"],
        b * e["e_end"],
        k * e["e_end"],
    )
    scale_f = jnp.exp(e["ending"])
    dah_l, drh_l, dbi_l, dki_l, dbe_l, dke_l, dv_l, dend_l = ([] for _ in range(8))
    for h in range(width // HEAD):
        lanes = slice(h * HEAD, (h + 1) * HEAD)
        ah, rh, bi, ki, be, ke, vh, _ = (
            x[:, lanes] for x in (ah_f, rh_f, bi_f, ki_f, be_f, ke_f, v, scale_f)
        )
        g = g_ref[:, lanes]
        p = dict(
            inverse=saved_ref[h, :, :tokens],
            ak=saved_ref[h, :, tokens : 2 * tokens],
            rb=saved_ref[h, :, 2 * tokens : 3 * tokens],
            reads=saved_ref[h, :, 2 * tokens : 4 * tokens],
        )
        u = saved_ref[h, :, 4 * tokens : 4 * tokens + HEAD]
        w = saved_ref[h, :, 4 * tokens + HEAD :]
        p["uv"] = jnp.concatenate([u, vh], axis=0)
        starts = [initial_ref[h]]
        for c in range(chunks - 1):
            starts.append(mm(starts[c], tf_ref[h, c, :, :HEAD]) + tf_ref[h, c, :, HEAD:])
        grad = jnp.zeros((HEAD, HEAD), F32)
        for m in got:
            grad = mm(grad, m[h, :, HEAD:].astype(F32), NT) + m[h, :, :HEAD].astype(F32)
        nexts = [None] * chunks
        for c in reversed(range(chunks)):
            nexts[c] = grad
            if c:
                s = slice(c * chunk, (c + 1) * chunk)
                grad = mm(grad, tf_ref[h, c, :, :HEAD], NT) + mm(g[s], rd_ref[s, lanes], TN)
        dw, du, dv, dbe, dke, dreader, dend = ([] for _ in range(7))
        for c in range(chunks):
            s = slice(c * chunk, (c + 1) * chunk)
            dt = mm1(starts[c], nexts[c], TN)
            df = nexts[c]
            dreader.append(mm1(g[s], starts[c]))
            dw.append(mm1(be[s], dt, NT))
            du.append(mm1(be[s], df, NT))
            dv.append(mm1(ke[s], df, NT))
            dbe.append(mm(w[s], dt) + mm(u[s], df))
            dke.append(mm(vh[s], df))
            line = jnp.sum(jnp.where(r64 == c64, dt, 0.0), axis=0, keepdims=True)
            dend.append(jnp.broadcast_to(line, (chunk, HEAD)))
        dw, du, dv, dbe, dke, dreader, dend = (
            jnp.concatenate(x, axis=0) for x in (dw, du, dv, dbe, dke, dreader, dend)
        )
        dreads = mm1(g, p["uv"], NT)
        drb = jnp.where(inclusive, mm1(dreader, w, NT) + dreads[:, :tokens], 0.0)
        drk = jnp.where(inclusive, dreads[:, tokens:], 0.0)
        duv = mm1(p["reads"], g, TN)
        dw = dw + mm1(p["rb"], dreader, TN)
        du = du + duv[:tokens]
        dz = mm1(p["inverse"], du, TN)
        q = mm1(p["inverse"], dw, TN)
        dsolve = mm1(dz, p["uv"], NT)
        dab = jnp.where(strict, mm1(q, w, NT) + dsolve[:, :tokens], 0.0)
        dak = jnp.where(strict, dsolve[:, tokens:], 0.0)
        dv = dv + duv[tokens:] + mm1(p["ak"], dz, TN)
        dpairs = jnp.concatenate(
            [jnp.concatenate([dab, dak], axis=1), jnp.concatenate([drb, drk], axis=1)], axis=0
        )
        dleft = mm(dpairs, jnp.concatenate([bi, ki], axis=0))
        dright = mm(dpairs, jnp.concatenate([ah, rh], axis=0), TN)
        dah_l.append(q + dleft[:tokens])
        drh_l.append(dreader + dleft[tokens:])
        dbi_l.append(dright[:tokens])
        dki_l.append(dright[tokens:])
        dbe_l.append(dbe)
        dke_l.append(dke)
        dv_l.append(dv)
        dend_l.append(dend)
    dah, drh, dbi, dki, dbe, dke, dv, dend = (
        jnp.concatenate(x, axis=1)
        for x in (dah_l, drh_l, dbi_l, dki_l, dbe_l, dke_l, dv_l, dend_l)
    )
    da = dah * e["e_before"]
    dr = drh * e["e_total"] + recept_ref[...]
    db = dbi * e["e_back"] + dbe * e["e_end"]
    dk = dki * e["e_back"] + dke * e["e_end"] + key_ref[...]
    dv = dv + value_ref[...]
    dbefore = dah * ah_f
    at_end = dbe * be_f + dke * ke_f
    dtotal = dbefore + drh * rh_f - dbi * bi_f - dki * ki_f - at_end
    dl = cumulate(inclusive, dtotal, TN) - dbefore + cumulate(same, at_end) + dend * scale_f
    table = raws[6]
    key_raw, rate, mixing, unit = (raw["key_raw"], raw["rate"], raw["mixing"], raw["unit"])
    ddecay = dl * (-DECAY_SCALE) * raw["decay_gate"] * (1.0 - raw["decay_gate"])
    dslope = dk * key_raw
    dlearn = (db * unit + dslope * table[12:13]) * rate * (1.0 - rate)
    dmix = dv * raw["gap"] * mixing * (1.0 - mixing)
    dunit = db * rate - da
    dscaled = raw["size"] * (dunit - unit * head_sums(dunit * unit))
    first_ref[...] = dv * mixing
    dr_ref[...] = dr.astype(BF16)
    dk_ref[...] = (dscaled * table[11:12] + dk * raw["slope"]).astype(BF16)
    dv_ref[...] = (dv * (1.0 - mixing)).astype(BF16)
    ddecay_ref[...] = ddecay.astype(BF16)
    dlearn_ref[...] = dlearn.astype(BF16)
    dmix_ref[...] = dmix.astype(BF16)
    table_ref[0:1] = token_sum(ddecay)
    table_ref[1:2] = token_sum(dlearn)
    table_ref[2:3] = token_sum(dmix)
    table_ref[3:4] = token_sum(dscaled * key_raw)
    table_ref[4:5] = token_sum(dslope * (rate - 1.0))


RAWS = 8


def chunk_of(tokens):
    return min(tokens, CHUNK)


def pairs_of(channels):
    return 2 if channels % (2 * HEAD) == 0 else channels // HEAD


def wkv_call(kernel, channels, inputs, outs):
    group = pairs_of(channels)
    width = group * HEAD

    def spec(shape):
        if len(shape) == 2:
            return pl.BlockSpec((shape[0], width), lambda i: (0, i))
        rest = tuple(shape[1:])
        return pl.BlockSpec((group,) + rest, lambda i: (i,) + (0,) * len(rest))

    return pl.pallas_call(
        kernel,
        grid=(channels // width,),
        in_specs=[spec(x.shape) for x in inputs],
        out_specs=[spec(s) for s, _ in outs],
        out_shape=[jax.ShapeDtypeStruct(s, d) for s, d in outs],
        interpret=INTERPRET,
    )(*inputs)


def wkv_local(raws):
    tokens, channels = raws[0].shape
    heads, chunk = (channels // HEAD, chunk_of(tokens))
    return wkv_call(
        functools.partial(local_kernel, chunk),
        channels,
        raws,
        [
            ((heads, tokens // chunk, HEAD, 2 * HEAD), F32),
            ((tokens, channels), F32),
            ((tokens, channels), F32),
            ((heads, HEAD, 2 * HEAD), BF16),
            ((heads, tokens, 4 * tokens + 2 * HEAD), F32),
        ],
    )


def wkv_outputs(got, raws, tf, reader, base, gates):
    tokens, channels = reader.shape
    heads, chunk = (channels // HEAD, chunk_of(tokens))
    return wkv_call(
        functools.partial(outputs_kernel, len(got), chunk),
        channels,
        [*got, *raws, tf, reader, base, gates],
        [
            ((tokens, channels), F32),
            ((tokens, channels), BF16),
            ((heads, HEAD, HEAD), F32),
        ],
    )


def wkv_local_back(raws, tf, reader, upper, memory, gates, sent):
    tokens, channels = reader.shape
    return wkv_call(
        functools.partial(local_back_kernel, chunk_of(tokens)),
        channels,
        [*raws, tf, reader, upper, memory, gates, sent],
        [(sent.shape, BF16)]
        + [((tokens, channels), F32)] * 4
        + [((tokens, channels), BF16), ((3, channels), F32)],
    )


def wkv_back(got, raws, initial, tf, reader, grad, saved, parts):
    tokens, channels = reader.shape
    return wkv_call(
        functools.partial(back_kernel, len(got), chunk_of(tokens)),
        channels,
        [*got, *raws, initial, tf, reader, grad, saved, *parts],
        [
            *[((tokens, channels), BF16)] * 6,
            ((tokens, channels), F32),
            ((5, channels), F32),
        ],
    )


def state_exchange(values, distance_sign):
    size = lax.axis_size("seq")
    return [
        lax.ppermute(values, "seq", shifted_route("seq", distance_sign * distance))
        for distance in range(size - 1, 0, -1)
    ]


def body(
    layer_input,
    first_layer_value,
    cotangent,
    receptance_weight,
    key_weight,
    value_weight,
    output_weight,
    channel_key_weight,
    channel_value_weight,
    decay_second_factor,
    learn_second_factor,
    residual_second_factor,
    gate_second_factor,
    decay_first_factor,
    learn_first_factor,
    residual_first_factor,
    gate_first_factor,
    vectors,
):
    sequences, tokens, features = layer_input.shape
    assert sequences == 1
    channels = first_layer_value.shape[2]
    hidden_units = channel_key_weight.shape[1]
    seq_size, seq_place = (lax.axis_size("seq"), lax.axis_index("seq"))
    head_size, head_place = (lax.axis_size("head"), lax.axis_index("head"))
    offset = head_place * channels
    share = features // seq_size
    small_share = features // (seq_size * head_size)

    x_bf = layer_input.reshape(tokens, features)
    x_rows = x_bf.astype(F32)
    cot_bf = cotangent.reshape(tokens, features)
    previous_x = lax.ppermute(x_bf[-1:], "seq", shifted_route("seq", 1)).astype(F32)
    has_previous = (seq_place > 0).astype(F32)

    firsts = (decay_first_factor, learn_first_factor, residual_first_factor, gate_first_factor)
    ranks = [member.shape[1] for member in firsts]
    columns = vectors.shape[1]
    small = jnp.concatenate(firsts + split_three(vectors), axis=1)
    seconds = (
        decay_second_factor,
        learn_second_factor,
        residual_second_factor,
        gate_second_factor,
    )
    second_rows = [member.shape[0] for member in seconds]
    payload = stack(
        [receptance_weight, key_weight, value_weight, output_weight.T, *seconds], 0
    )
    gathered = lax.all_gather(payload, "seq", axis=0, tiled=False)
    cuts = []
    at = 0
    for rows in [share] * 4 + second_rows:
        cuts.append(gathered[:, at : at + rows].reshape(seq_size * rows, channels))
        at += rows
    recept_cols, key_cols, value_cols, out_cols, decay_up, learn_up, mix_up, gate_up = cuts

    shared = lax.all_to_all(
        jnp.concatenate([share_out(standardize(x_rows).astype(BF16)), share_out(cot_bf)], axis=2),
        "seq",
        split_axis=0,
        concat_axis=0,
        tiled=True,
    )
    standard_all = shared[..., :share].reshape(seq_size * tokens, share)
    cot_all = shared[..., share:].reshape(seq_size * tokens, share)

    small_all = permute_gather(after(small, payload), "seq")
    small_all = permute_gather(small_all, "head")
    small_all = (
        small_all.reshape(head_size, seq_size, small_share, -1)
        .transpose(1, 0, 2, 3)
        .reshape(features, -1)
    )
    downs = []
    at = 0
    for rank in ranks:
        downs.append(small_all[:, at : at + rank])
        at += rank
    decay_down, learn_down, mix_down, gate_down = downs
    pieces = small_all[:, at : at + 3 * columns].astype(F32)
    vec = (
        pieces[:, :columns] + pieces[:, columns : 2 * columns] + pieces[:, 2 * columns :]
    ).T
    local_vec = lax.dynamic_slice_in_dim(vec, offset, channels, 1)

    ffn_payload = after(
        jnp.concatenate([channel_key_weight, channel_value_weight.T], axis=1), shared
    )
    ffn_gathered = lax.all_gather(ffn_payload, "seq", axis=0, tiled=True)
    ffn_key_cols = ffn_gathered[:, :hidden_units]
    ffn_value_cols = ffn_gathered[:, hidden_units:]

    def first_norm(values, table):
        return layer_norm(values, table[0], table[1])

    def second_norm(values, table):
        return layer_norm(values, table[16], table[17])

    def time_inputs(normed, previous, table):
        return shift_mix(normed, previous, table[2:8])

    def ffn_inputs(normed, previous, table):
        return shift_mix(normed, previous, table[18:19])[0]

    normed_a = first_norm(x_rows, vec)
    prev_a = first_norm(previous_x, vec) * has_previous
    mixes = time_inputs(normed_a, prev_a, vec)
    mixed_recept, mixed_decay, mixed_key, mixed_value, mixed_learn, mixed_gate = mixes
    recept = narrow_dot(mixed_recept, recept_cols)
    key_raw = narrow_dot(mixed_key, key_cols)
    value_raw = narrow_dot(mixed_value, value_cols)
    decay_low = narrow_dot(mixed_decay, decay_down)
    learn_low = narrow_dot(mixed_learn, learn_down)
    mix_low = narrow_dot(mixed_value, mix_down)
    gate_low = narrow_dot(mixed_gate, gate_down)
    decay_tanh = jnp.tanh(decay_low)
    gate_sigm = jax.nn.sigmoid(gate_low)
    decay_shift = narrow_dot(decay_tanh, decay_up)
    learn_shift = narrow_dot(learn_low, learn_up)
    mix_shift = narrow_dot(mix_low, mix_up)
    gates = narrow_dot(gate_sigm, gate_up)
    first_value = first_layer_value.reshape(tokens, channels)
    raws = (
        key_raw, value_raw, decay_shift, learn_shift, mix_shift, first_value, local_vec, recept
    )
    states, reader, base, sent, saved = wkv_local(raws)
    memory_out, pre_out, initial = wkv_outputs(
        state_exchange(sent, 1), raws, states, reader, base, gates
    )
    middle = x_rows + head_sum(narrow_nt(pre_out, out_cols))
    normed_b, norm_b_back = jax.vjp(second_norm, middle, vec)
    prev_b = lax.ppermute(normed_b[-1:], "seq", shifted_route("seq", 1))
    mixed_ffn, ffn_back = jax.vjp(ffn_inputs, normed_b, prev_b, vec)
    middle_share = lax.dynamic_slice_in_dim(middle, offset, channels, 1)
    hidden_pre = narrow_dot(mixed_ffn, ffn_key_cols)
    active = jnp.maximum(hidden_pre, 0.0)
    hidden = active * active
    result = middle_share + head_scatter(narrow_nt(hidden, ffn_value_cols))
    pre_grad = narrow_dot(cot_bf, ffn_value_cols) * 2.0 * active
    ffn_rows = lax.all_gather(
        jnp.concatenate([member.astype(BF16) for member in (hidden, pre_grad, pre_out)], axis=1),
        "seq",
        axis=0,
        tiled=True,
    )
    ffn_back_part = narrow_nt(pre_grad, ffn_key_cols)
    normed_b_grad, prev_b_grad, vec_ffn_mix = ffn_back(ffn_back_part)
    returned_b = lax.ppermute(prev_b_grad, "seq", shifted_route("seq", -1))
    normed_b_grad = jnp.concatenate([normed_b_grad[:-1], normed_b_grad[-1:] + returned_b], axis=0)
    middle_part, vec_ffn_norm = norm_b_back(normed_b_grad)
    middle_grad = cot_bf.astype(F32) + head_sum(middle_part)
    middle_grad_share = lax.dynamic_slice_in_dim(middle_grad, offset, channels, 1)
    pre_out_grad = narrow_dot(middle_grad, out_cols)
    sent_back, memory_grad, recept_part, key_part, value_part, gate_grad, table_out = (
        wkv_local_back(raws, states, reader, pre_out_grad, memory_out, gates, sent)
    )
    grad_gate_up = narrow_tn(gate_sigm, gate_grad)
    gate_low_grad = narrow_nt(gate_grad, gate_up) * gate_sigm * (1.0 - gate_sigm)
    later = state_exchange(sent_back, -1)
    shares = stack([share_out(mixed_ffn.astype(BF16)), share_out(middle_grad.astype(BF16))], 1)
    middle_shared = lax.all_to_all(shares, "seq", split_axis=0, concat_axis=0, tiled=True)
    *row_grads, first_grad, table_param = wkv_back(
        later,
        raws,
        initial,
        states,
        reader,
        memory_grad,
        saved,
        (recept_part, key_part, value_part),
    )
    decay_shift_grad, learn_shift_grad, mix_shift_grad = row_grads[3:]
    decay_low_grad = narrow_nt(decay_shift_grad, decay_up) * (1.0 - decay_tanh * decay_tanh)
    learn_low_grad = narrow_nt(learn_shift_grad, learn_up)
    mix_low_grad = narrow_nt(mix_shift_grad, mix_up)
    low_grad = head_sum(
        jnp.concatenate([decay_low_grad, learn_low_grad, mix_low_grad, gate_low_grad], axis=1)
    )
    final = jnp.concatenate(
        [*row_grads[:3], low_grad.astype(BF16)], axis=1
    )
    sent_final = after(final, ffn_rows)
    final = lax.all_gather(sent_final, "seq", axis=0, tiled=True)
    second_grads = (
        narrow_tn(decay_tanh, after(decay_shift_grad, sent_final)),
        narrow_tn(learn_low, after(learn_shift_grad, sent_final)),
        narrow_tn(mix_low, after(mix_shift_grad, sent_final)),
        grad_gate_up,
    )
    second_parts = []
    for member, rows in zip(second_grads, second_rows):
        member = member.astype(BF16).reshape(seq_size, rows, channels)
        second_parts += [member[..., at : at + share] for at in range(0, channels, share)]
    recept_sent, key_sent, value_sent = (
        sent_final[:, c * channels : (c + 1) * channels] for c in range(3)
    )
    mixes_grad = (
        narrow_nt(recept_sent, recept_cols),
        narrow_nt(after(decay_low_grad, sent_final), decay_down),
        narrow_nt(key_sent, key_cols),
        narrow_nt(value_sent, value_cols) + narrow_nt(after(mix_low_grad, sent_final), mix_down),
        narrow_nt(after(learn_low_grad, sent_final), learn_down),
        narrow_nt(after(gate_low_grad, sent_final), gate_down),
    )
    _, mix_back = jax.vjp(time_inputs, normed_a, prev_a, vec)
    normed_a_grad, prev_a_grad, vec_attn_mix = mix_back(mixes_grad)
    returned_a = lax.ppermute(prev_a_grad, "seq", shifted_route("seq", -1))
    normed_a_grad = jnp.concatenate([normed_a_grad[:-1], normed_a_grad[-1:] + returned_a], axis=0)
    _, norm_a_back = jax.vjp(first_norm, x_rows, vec)
    input_part, vec_attn_norm = norm_a_back(normed_a_grad)
    input_grad = middle_grad_share + head_scatter(input_part)

    table_local = jnp.concatenate([table_param, table_out], axis=0)
    vec_grad = lax.dynamic_update_slice(
        vec_ffn_mix + vec_ffn_norm + vec_attn_mix + vec_attn_norm, table_local, (8, offset)
    )
    vec_split = vec_grad.reshape(columns, seq_size, share).transpose(1, 0, 2)
    vec_high, vec_low, _ = split_three(vec_split)
    last = lax.all_to_all(
        stack(
            [*second_parts, vec_high, vec_low],
            1,
        ),
        "seq",
        split_axis=0,
        concat_axis=0,
        tiled=True,
    )
    mixed_all = middle_shared[:, :tokens].reshape(seq_size * tokens, share)
    middle_grad_all = middle_shared[:, tokens:].reshape(seq_size * tokens, share)
    sums = jnp.sum(last.astype(F32), axis=0)
    second_sum = sums[: -2 * columns]
    vec_seq = sums[-2 * columns : -columns] + sums[-columns:]
    vec_mine = head_scatter(vec_seq, F32).T

    share_vec = lax.dynamic_slice_in_dim(vec, seq_place * share, share, 1)
    normed_all = standard_all.astype(F32) * share_vec[0] + share_vec[1]
    zero_row = jnp.zeros((1, share), F32)
    recept_all, decay_all, key_all, value_all, learn_all, gate_all = shift_mix(
        normed_all, zero_row, share_vec[2:8]
    )
    grad_recept = narrow_tn(recept_all, final[:, :channels])
    grad_key = narrow_tn(key_all, final[:, channels : 2 * channels])
    grad_value = narrow_tn(value_all, final[:, 2 * channels : 3 * channels])
    first_outs = []
    at = 3 * channels
    for member, rank in zip((decay_all, learn_all, value_all, gate_all), ranks):
        mine = lax.dynamic_slice_in_dim(member, head_place * small_share, small_share, 1)
        first_outs.append(narrow_tn(mine, final[:, at : at + rank]))
        at += rank

    hidden_all = ffn_rows[:, :hidden_units]
    pre_grad_all = ffn_rows[:, hidden_units : 2 * hidden_units]
    pre_out_all = ffn_rows[:, 2 * hidden_units :]
    second_outs = []
    at = 0
    for rows in second_rows:
        parts = []
        for _ in range(0, channels, share):
            parts.append(second_sum[at : at + rows])
            at += rows
        second_outs.append(jnp.concatenate(parts, axis=1))
    return (
        result[None],
        input_grad[None],
        first_grad[None],
        grad_recept,
        grad_key,
        grad_value,
        narrow_tn(pre_out_all, middle_grad_all),
        narrow_tn(mixed_all, pre_grad_all),
        narrow_tn(hidden_all, cot_all),
        *second_outs,
        *first_outs,
        vec_mine,
    )


def solution(mesh):
    placed = (
        P(None, "seq", None),
        P(None, "seq", "head"),
        P(None, "seq", None),
        P("seq", "head"),
        P("seq", "head"),
        P("seq", "head"),
        P("head", "seq"),
        P("seq", "head"),
        P("head", "seq"),
        P("seq", "head"),
        P("seq", "head"),
        P("seq", "head"),
        P("seq", "head"),
        P(("seq", "head"), None),
        P(("seq", "head"), None),
        P(("seq", "head"), None),
        P(("seq", "head"), None),
        P(("seq", "head"), None),
    )
    return jax.shard_map(
        body,
        mesh=mesh,
        in_specs=placed,
        out_specs=(
            P(None, "seq", "head"),
            P(None, "seq", "head"),
            P(None, "seq", "head"),
            P("seq", "head"),
            P("seq", "head"),
            P("seq", "head"),
            P("head", "seq"),
            P("seq", "head"),
            P("head", "seq"),
            P("seq", "head"),
            P("seq", "head"),
            P("seq", "head"),
            P("seq", "head"),
            P(("seq", "head"), None),
            P(("seq", "head"), None),
            P(("seq", "head"), None),
            P(("seq", "head"), None),
            P(("seq", "head"), None),
        ),
        check_vma=False,
    )
```
